32 devices in a mesh: dp: 2 (over core), seq: 4 (over y, x), heads: 4 (over z).
Axes of the slice: x: 2, y: 2, z: 4, core: 2. Of those that a mesh axis runs over, the one named last changes fastest.
Arguments:
- residual: bfloat16 [6, 1536, 1536], P('dp', ('seq', 'heads')), may hold values from -6 to 6
- out_grad: bfloat16 [6, 1536, 1536], P('dp', 'seq'), may hold values from -6 to 6
- lengths: int32 [6], P('dp'), may hold values from 384 to 1536, as said below
- attn_gain: bfloat16 [1536], replicated, may hold values from 0.25 to 1.75
- query_weight: bfloat16 [1536, 1536], P(None, 'heads'), may hold values from -0.21875 to 0.21875
- query_bias: bfloat16 [1536], P('heads'), may hold values from -4 to 4
- key_weight: bfloat16 [1536, 256], replicated, may hold values from -0.21875 to 0.21875
- key_bias: bfloat16 [256], replicated, may hold values from -4 to 4
- value_weight: bfloat16 [1536, 256], replicated, may hold values from -0.15625 to 0.15625
- value_bias: bfloat16 [256], replicated, may hold values from -4 to 4
- output_weight: bfloat16 [1536, 1536], P('heads'), may hold values from -0.4375 to 0.4375
- ffn_gain: bfloat16 [1536], replicated, may hold values from 0.25 to 1.75
- gate_weight: bfloat16 [1536, 8960], P(('dp', 'seq'), 'heads'), may hold values from -0.15625 to 0.15625
- up_weight: bfloat16 [1536, 8960], P(('dp', 'seq'), 'heads'), may hold values from -0.15625 to 0.15625
- down_weight: bfloat16 [8960, 1536], P('heads', ('dp', 'seq')), may hold values from -0.0625 to 0.0625
Outputs:
- block_out: bfloat16 [6, 1536, 1536], P('dp', ('seq', 'heads'))
- residual_grad: float32 [6, 1536, 1536], P('dp', ('seq', 'heads'))
- attn_gain_grad: float32 [1536], P(('dp', 'seq', 'heads'))
- query_weight_grad: float32 [1536, 1536], P(('dp', 'seq'), 'heads')
- query_bias_grad: float32 [1536], P('heads')
- key_weight_grad: float32 [1536, 256], P(('dp', 'seq'), 'heads')
- key_bias_grad: float32 [256], P('heads')
- value_weight_grad: float32 [1536, 256], P(('dp', 'seq'), 'heads')
- value_bias_grad: float32 [256], P('heads')
- output_weight_grad: float32 [1536, 1536], P('heads', ('dp', 'seq'))
- ffn_gain_grad: float32 [1536], P(('dp', 'seq', 'heads'))
- gate_weight_grad: float32 [1536, 8960], P(('dp', 'seq'), 'heads')
- up_weight_grad: float32 [1536, 8960], P(('dp', 'seq'), 'heads')
- down_weight_grad: float32 [8960, 1536], P('heads', ('dp', 'seq'))
The draws below stay inside these ranges and needn't reach their ends.
Inputs may be any that keep to these rules, and one draw needn't show every extreme that they name: `lengths`: each row is valid up to its length and padded after it; at least one row has length exactly 1536.
All inputs are finite; a program needn't handle non-finite values.
Results may differ from the reference program's by a relative error of at most 0.019.
Values may be sent and summed in bfloat16 or wider, within the bound.
No kernel may reach another device: no remote copies, remote signals or barrier semaphores. Data moves between devices by JAX's collectives and lax.ppermute only.
A program may use at most 256 MiB of HBM per device.

```python
import jax
import jax.numpy as jnp
from jax import lax

D = 1536
FF = 8960
H = 12
KVH = 2
HD = 128
LEN = 1536
ROWS = 6


def draw_lengths(key, part):
    base = jax.random.randint(key, (ROWS,), LEN // 4, LEN + 1)
    chosen = jax.random.randint(jax.random.fold_in(key, 7), (), 0, ROWS)
    return jnp.where(jnp.arange(ROWS) == chosen, LEN, base).astype(jnp.int32)


def block_levels(stream_key, extent, shards, least, largest):
    level = 1.0
    for axis_at, parts in shards:
        steps = jax.random.uniform(jax.random.fold_in(jax.random.fold_in(stream_key, 6), axis_at), (parts,), jnp.float32, least / len(shards), largest / len(shards))
        level = level * jnp.repeat(jnp.exp(steps), extent[axis_at] // parts).reshape((-1,) + (1,) * (len(extent) - 1 - axis_at))
    return level


def scatter_about(rng, extent, deviation, most, pieces=(), kind=jnp.bfloat16):
    entries = deviation * jax.random.normal(rng, extent, jnp.float32)
    if pieces:
        entries = entries * block_levels(rng, extent, pieces, -0.22, 0.18)
    return jnp.clip(entries, -most, most).astype(kind)


def setup_inputs(seed: int = 0) -> dict:
    key_of = jax.random.split(jax.random.key(seed), 16)
    return {
        "residual": scatter_about(key_of[0], (ROWS, LEN, D), 1.0, 6.0, ((0, 2), (1, 16))),
        "out_grad": scatter_about(key_of[1], (ROWS, LEN, D), 1.0, 6.0, ((0, 2), (1, 4))),
        "lengths": draw_lengths(jax.random.fold_in(key_of[15], 71), 0),
        "attn_gain": jnp.clip(1.0 + 0.15 * jax.random.normal(key_of[3], (D,), jnp.float32), 0.25, 1.75).astype(jnp.bfloat16),
        "query_weight": scatter_about(key_of[4], (D, H * HD), (D // 2) ** -0.5, 0.21875, ((1, 4),)),
        "query_bias": scatter_about(key_of[5], (H * HD,), 0.6, 4.0, ((0, 4),)),
        "key_weight": scatter_about(key_of[6], (D, KVH * HD), (D // 2) ** -0.5, 0.21875),
        "key_bias": scatter_about(key_of[7], (KVH * HD,), 0.6, 4.0),
        "value_weight": scatter_about(key_of[8], (D, KVH * HD), D ** -0.5, 0.15625),
        "value_bias": scatter_about(key_of[9], (KVH * HD,), 0.6, 4.0),
        "output_weight": scatter_about(key_of[10], (H * HD, D), (H * HD // 8) ** -0.5, 0.4375, ((0, 4),)),
        "ffn_gain": jnp.clip(1.0 + 0.15 * jax.random.normal(key_of[11], (D,), jnp.float32), 0.25, 1.75).astype(jnp.bfloat16),
        "gate_weight": scatter_about(key_of[12], (D, FF), D ** -0.5, 0.15625, ((0, 8), (1, 4))),
        "up_weight": scatter_about(key_of[13], (D, FF), D ** -0.5, 0.15625, ((0, 8), (1, 4))),
        "down_weight": scatter_about(key_of[14], (FF, D), FF ** -0.5, 0.0625, ((0, 4), (1, 8))),
    }


epsilon = 1e-06
rope_base = 1000000.0
masked_value = -1000000000.0
highest = lax.Precision.HIGHEST

@jax.custom_vjp
def low(v):
    return lax.optimization_barrier(v.astype(jnp.bfloat16)).astype(jnp.float32)

@jax.custom_vjp
def low_back(v):
    return v

def low_keep(v):
    return (low(v), None)

def low_pass(kept, grad):
    return (grad,)

def back_keep(v):
    return (v, None)

def back_low(kept, grad):
    return (low(grad),)
low.defvjp(low_keep, low_pass)
low_back.defvjp(back_keep, back_low)

def matmul(left, right):
    return jnp.dot(left, right, precision=highest, preferred_element_type=jnp.float32)

def rms_scale(values):
    return lax.rsqrt(lax.optimization_barrier(jnp.mean(values * values, axis=-1, keepdims=True)) + epsilon)

def rotate(values):
    middle = values.shape[-1] // 2
    return jnp.concatenate([-values[..., middle:], values[..., :middle]], axis=-1)

def angles(positions, head_size):
    inverse_freq = rope_base ** (-jnp.arange(0, head_size // 2, dtype=jnp.float32) * 2.0 / head_size)
    phase_grid = positions[:, None] * inverse_freq[None, :]
    phase_grid = jnp.concatenate([phase_grid, phase_grid], axis=-1)
    return (jnp.cos(phase_grid), jnp.sin(phase_grid))

def one_row(stream, length, params):
    attn_gain, query_weight, query_bias, key_weight, key_bias, value_weight, value_bias, output_weight, ffn_gain, gate_weight, up_weight, down_weight = params
    cosine, sine = angles(jnp.arange(LEN, dtype=jnp.float32), HD)
    normed1 = stream * rms_scale(stream)
    input1 = low(normed1 * attn_gain)
    query = low_back(matmul(input1, query_weight) + query_bias).reshape(LEN, H, HD).transpose(1, 0, 2)
    keys = low_back(matmul(input1, key_weight) + key_bias).reshape(LEN, KVH, HD).transpose(1, 0, 2)
    values = low(low_back(matmul(input1, value_weight) + value_bias)).reshape(LEN, KVH, HD).transpose(1, 0, 2)
    query = low(query * cosine + rotate(query) * sine)
    keys = low(keys * cosine + rotate(keys) * sine)
    keys = jnp.repeat(keys, H // KVH, axis=0)
    values = jnp.repeat(values, H // KVH, axis=0)
    block = min(512, LEN)
    count = LEN // block
    query_blocks = query.reshape(H, count, block, HD).transpose(1, 0, 2, 3)
    starts = jnp.arange(count, dtype=jnp.int32) * block
    key_pos = jnp.arange(LEN, dtype=jnp.int32)
    score_scale = HD ** (-0.5)

    def attend(items):
        query_block, start = items
        query_pos = start + jnp.arange(block, dtype=jnp.int32)
        unscaled_scores = low_back(jnp.einsum('hqd,hkd->hqk', query_block, keys, precision=highest))
        visible = (key_pos[None, :] <= query_pos[:, None]) & (key_pos[None, :] < length)
        logits = jnp.where(visible[None], unscaled_scores * score_scale, masked_value)
        probs = low(jax.nn.softmax(logits, axis=-1))
        return jnp.einsum('hqk,hkd->hqd', probs, values, precision=highest)
    blocks_out = lax.map(jax.checkpoint(attend), (query_blocks, starts))
    attended = blocks_out.transpose(0, 2, 1, 3).reshape(LEN, H * HD)
    attended = low(low_back(attended))
    stream2 = stream + low_back(matmul(attended, output_weight))
    normed2 = stream2 * rms_scale(stream2)
    input2 = low(normed2 * ffn_gain)
    gate = low_back(matmul(input2, gate_weight))
    up_act = low_back(matmul(input2, up_weight))
    hidden = low(jax.nn.silu(gate) * up_act)
    return stream2 + matmul(hidden, down_weight)

def reference(residual, out_grad, lengths, attn_gain, query_weight, query_bias, key_weight, key_bias, value_weight, value_bias, output_weight, ffn_gain, gate_weight, up_weight, down_weight):
    params = tuple((item.astype(jnp.float32) for item in (attn_gain, query_weight, query_bias, key_weight, key_bias, value_weight, value_bias, output_weight, ffn_gain, gate_weight, up_weight, down_weight)))

    def step(totals, items):
        row_in, row_grad, length = items
        result, pull = jax.vjp(lambda row_value, row_params: one_row(row_value, length, row_params), row_in.astype(jnp.float32), params)
        grad_in, grad_params = pull(row_grad.astype(jnp.float32))
        totals = jax.tree.map(lambda first, second: first + second, totals, grad_params)
        return (totals, (result.astype(jnp.bfloat16), grad_in))
    zeros = jax.tree.map(jnp.zeros_like, params)
    totals, (outputs, grads) = lax.scan(step, zeros, (residual, out_grad, lengths))
    return (outputs, grads, totals[0], totals[1], totals[2], totals[3], totals[4], totals[5], totals[6], totals[7], totals[8], totals[9], totals[10], totals[11])
```

```python
import jax
import jax.numpy as jnp
from jax import lax
from jax.experimental import pallas as pl
from jax.experimental.pallas import tpu as pltpu
from jax.sharding import PartitionSpec as P

H = 12
KVH = 2
HD = 128

epsilon = 1e-06
rope_base = 1000000.0
hidden_logit = -1e30
log2_e = 1.4426950408889634

bf16 = jnp.bfloat16
f32 = jnp.float32
vmem_bytes = 48 * 2**20


def swap(value, axis, mask):
    pairs = [(source, source ^ mask) for source in range(lax.axis_size(axis))]
    return lax.ppermute(value, axis, pairs)


def rotate_down(value, axis):
    size = lax.axis_size(axis)
    pairs = [(source, (source - 1) % size) for source in range(size)]
    return lax.ppermute(value, axis, pairs)


def add_low(first, second):
    return (first.astype(f32) + second.astype(f32)).astype(bf16)


def join(parts, dim):
    return parts[0] if len(parts) == 1 else jnp.concatenate(parts, axis=dim)


def split(value, count, dim):
    return [value] if count == 1 else jnp.split(value, count, axis=dim)


def seq_masks():
    bits = lax.axis_size("seq").bit_length() - 1
    ahead = [1 << bit for bit in range(bits)]
    return ahead, ahead[bits // 2 :] + ahead[: bits // 2]


def gather_seq(block, masks, dim):
    held = {0: block}
    for mask in masks:
        keys = list(held)
        came = split(swap(join([held[k] for k in keys], dim), "seq", mask), len(keys), dim)
        held.update({k ^ mask: piece for k, piece in zip(keys, came)})
    return [held[r] for r in range(len(held))]


def scatter_seq(blocks, masks, dim):
    held = dict(enumerate(blocks))
    for mask in masks:
        away = [k for k in held if k & mask]
        came = split(swap(join([held[k] for k in away], dim), "seq", mask), len(away), dim)
        for k, piece in zip(away, came):
            held[k ^ mask] = add_low(held[k ^ mask], piece)
            del held[k]
    return held[0]


def gather_ring(block, axis):
    held = [block]
    for _ in range(lax.axis_size(axis) - 1):
        held.append(rotate_down(held[-1], axis))
    return held


def scatter_ring(blocks, axis):
    total = blocks[1]
    for block in blocks[2:] + blocks[:1]:
        total = add_low(rotate_down(total, axis), block)
    return total


def take(value, index, size, dim):
    return lax.dynamic_slice_in_dim(value, index * size, size, dim)


def turn(values, cosine, sine):
    return values * cosine + pltpu.roll(values, HD // 2, 1) * sine


def turn_back(values, cosine, sine):
    return values * cosine - pltpu.roll(values, HD // 2, 1) * sine


def first_kernel(x_ref, gain_ref, kw_ref, vw_ref, kb_ref, vb_ref, cos_ref, sin_ref, in_ref, kv_ref):
    x = x_ref[0].astype(f32)
    scale = lax.rsqrt(jnp.mean(x * x, axis=-1, keepdims=True) + epsilon)
    low = (x * scale * gain_ref[...].astype(f32)).astype(bf16)
    in_ref[0] = low
    width = kw_ref.shape[1]
    keys = jnp.dot(low, kw_ref[...], preferred_element_type=f32) + kb_ref[...].astype(f32)
    for at in range(0, width, HD):
        kv_ref[0, :, at : at + HD] = turn(
            keys[:, at : at + HD], cos_ref[...], sin_ref[...]
        ).astype(bf16)
    values = jnp.dot(low, vw_ref[...], preferred_element_type=f32) + vb_ref[...].astype(f32)
    kv_ref[0, :, width:] = values.astype(bf16)


def first_call(residual, gain, kw, vw, kb, vb, cosine, sine):
    rows, count, width = residual.shape
    kv = kw.shape[1]
    fixed = lambda shape: pl.BlockSpec(shape, lambda r: (0, 0))
    row = lambda size: pl.BlockSpec((1, count, size), lambda r: (r, 0, 0))
    return pl.pallas_call(
        first_kernel,
        grid=(rows,),
        in_specs=[
            row(width),
            fixed((1, width)),
            fixed((width, kv)),
            fixed((width, kv)),
            fixed((1, kv)),
            fixed((1, kv)),
            fixed((count, HD)),
            fixed((count, HD)),
        ],
        out_specs=[row(width), row(2 * kv)],
        out_shape=[
            jax.ShapeDtypeStruct((rows, count, width), bf16),
            jax.ShapeDtypeStruct((rows, count, 2 * kv), bf16),
        ],
        cost_estimate=pl.CostEstimate(
            flops=4 * rows * count * width * kv,
            bytes_accessed=2 * (2 * rows * count * width + 2 * width * kv),
            transcendentals=0,
        ),
        compiler_params=pltpu.CompilerParams(vmem_limit_bytes=vmem_bytes),
        name="first_norm",
    )(residual, gain[None], kw, vw, kb[None], vb[None], cosine, sine)


def attend_kernel(
    q_ref, cos_ref, sin_ref, k_ref, v_ref, kpos_ref, limit_ref, out_ref, turned_ref, log_ref
):
    count = q_ref.shape[1]
    heads = q_ref.shape[2] // HD
    turned = []
    for h in range(heads):
        u = turn(q_ref[0, :, h * HD : (h + 1) * HD], cos_ref[...], sin_ref[...])
        turned_ref[0, :, h * HD : (h + 1) * HD] = u.astype(bf16)
        turned.append(u)
    query = jnp.concatenate(turned, axis=0).astype(bf16)
    scores = lax.dot_general(
        k_ref[0], query, (((1,), (1,)), ((), ())), preferred_element_type=f32
    )
    seen = kpos_ref[...] <= limit_ref[0]
    scores = jnp.where(seen, scores * (HD**-0.5 * log2_e), hidden_logit)
    peak = jnp.max(scores, axis=0, keepdims=True)
    weight = jnp.exp2(scores - peak)
    total = jnp.sum(weight, axis=0, keepdims=True)
    log_ref[0, 0] = peak + jnp.log2(total)
    out = lax.dot_general(
        v_ref[0], weight.astype(bf16), (((0,), (0,)), ((), ())), preferred_element_type=f32
    )
    out = (out * (1.0 / total)).T
    for h in range(heads):
        out_ref[0, :, h * HD : (h + 1) * HD] = out[h * count : (h + 1) * count].astype(bf16)


def attend_call(query, cosine, sine, keys, values, kpos, limit):
    rows, count, width = query.shape
    length = keys.shape[1]
    groups = KVH
    wide = width // groups
    many = limit.shape[2]
    part = pl.BlockSpec((1, count, wide), lambda r, g: (r, 0, g))
    fixed = lambda shape: pl.BlockSpec(shape, lambda r, g: (0, 0))
    whole = pl.BlockSpec((1, length, HD), lambda r, g: (r, 0, g))
    work = rows * groups * length * many
    return pl.pallas_call(
        attend_kernel,
        grid=(rows, groups),
        in_specs=[
            part,
            fixed((count, HD)),
            fixed((count, HD)),
            whole,
            whole,
            fixed((length, 1)),
            pl.BlockSpec((1, 1, many), lambda r, g: (r, 0, 0)),
        ],
        out_specs=[part, part, pl.BlockSpec((1, 1, 1, many), lambda r, g: (r, g, 0, 0))],
        out_shape=[
            jax.ShapeDtypeStruct((rows, count, width), bf16),
            jax.ShapeDtypeStruct((rows, count, width), bf16),
            jax.ShapeDtypeStruct((rows, groups, 1, many), f32),
        ],
        cost_estimate=pl.CostEstimate(
            flops=4 * work * HD, bytes_accessed=4 * keys.size, transcendentals=work
        ),
        compiler_params=pltpu.CompilerParams(vmem_limit_bytes=vmem_bytes),
        name="attend",
    )(query, cosine, sine, keys, values, kpos, limit)


def attend_back_kernel(
    q_ref,
    og_ref,
    cos_ref,
    sin_ref,
    k_ref,
    v_ref,
    kpos_ref,
    limit_ref,
    log_ref,
    gq_ref,
    gk_ref,
    gv_ref,
):
    count = q_ref.shape[1]
    heads = q_ref.shape[2] // HD

    def rows_of(ref):
        parts = [ref[0, :, h * HD : (h + 1) * HD].astype(f32) for h in range(heads)]
        return jnp.concatenate(parts, axis=0).astype(bf16)

    query, upstream = rows_of(q_ref), rows_of(og_ref)
    last = (((1,), (1,)), ((), ()))
    scores = lax.dot_general(k_ref[0], query, last, preferred_element_type=f32)
    seen = kpos_ref[...] <= limit_ref[0]
    scale = HD**-0.5
    probs = jnp.exp2(jnp.where(seen, scores * (scale * log2_e) - log_ref[0, 0], hidden_logit))
    gv_ref[0] = jnp.dot(probs.astype(bf16), upstream, preferred_element_type=f32).astype(bf16)
    grad_probs = lax.dot_general(v_ref[0], upstream, last, preferred_element_type=f32)
    mixed = probs * grad_probs
    total = jnp.sum(mixed, axis=0, keepdims=True)
    grad_scores = ((mixed - probs * total) * scale).astype(bf16)
    gk_ref[0] = jnp.dot(grad_scores, query, preferred_element_type=f32).astype(bf16)
    grad_query = lax.dot_general(
        k_ref[0], grad_scores, (((0,), (0,)), ((), ())), preferred_element_type=f32
    ).T
    for h in range(heads):
        gq_ref[0, :, h * HD : (h + 1) * HD] = turn_back(
            grad_query[h * count : (h + 1) * count], cos_ref[...], sin_ref[...]
        ).astype(bf16)


def attend_back_call(query, upstream, cosine, sine, keys, values, kpos, limit, logs):
    rows, count, width = query.shape
    length = keys.shape[1]
    groups = KVH
    wide = width // groups
    many = limit.shape[2]
    part = pl.BlockSpec((1, count, wide), lambda r, g: (r, 0, g))
    fixed = lambda shape: pl.BlockSpec(shape, lambda r, g: (0, 0))
    whole = pl.BlockSpec((1, length, HD), lambda r, g: (r, 0, g))
    work = rows * groups * length * many
    return pl.pallas_call(
        attend_back_kernel,
        grid=(rows, groups),
        in_specs=[
            part,
            part,
            fixed((count, HD)),
            fixed((count, HD)),
            whole,
            whole,
            fixed((length, 1)),
            pl.BlockSpec((1, 1, many), lambda r, g: (r, 0, 0)),
            pl.BlockSpec((1, 1, 1, many), lambda r, g: (r, g, 0, 0)),
        ],
        out_specs=[part, whole, whole],
        out_shape=[
            jax.ShapeDtypeStruct((rows, count, width), bf16),
            jax.ShapeDtypeStruct((rows, length, groups * HD), bf16),
            jax.ShapeDtypeStruct((rows, length, groups * HD), bf16),
        ],
        cost_estimate=pl.CostEstimate(
            flops=10 * work * HD, bytes_accessed=8 * keys.size, transcendentals=work
        ),
        compiler_params=pltpu.CompilerParams(vmem_limit_bytes=vmem_bytes),
        name="attend_back",
    )(query, upstream, cosine, sine, keys, values, kpos, limit, logs)


def turn_back_kernel(kv_ref, cos_ref, sin_ref, out_ref):
    half = kv_ref.shape[2] // 2
    for at in range(0, half, HD):
        out_ref[0, :, at : at + HD] = turn_back(
            kv_ref[0, :, at : at + HD].astype(f32), cos_ref[...], sin_ref[...]
        ).astype(bf16)
    out_ref[0, :, half:] = kv_ref[0, :, half:]


def turn_back_call(kv, cosine, sine):
    rows, count, width = kv.shape
    row = pl.BlockSpec((1, count, width), lambda r: (r, 0, 0))
    table = pl.BlockSpec((count, HD), lambda r: (0, 0))
    return pl.pallas_call(
        turn_back_kernel,
        grid=(rows,),
        in_specs=[row, table, table],
        out_specs=row,
        out_shape=jax.ShapeDtypeStruct(kv.shape, bf16),
        cost_estimate=pl.CostEstimate(
            flops=4 * kv.size, bytes_accessed=4 * kv.size, transcendentals=0
        ),
        compiler_params=pltpu.CompilerParams(vmem_limit_bytes=vmem_bytes),
        name="turn_back",
    )(kv, cosine, sine)


def matmul(left, right):
    return jnp.dot(left, right, preferred_element_type=f32)


def matmul_nt(left, right):
    return lax.dot_general(left, right, (((1,), (1,)), ((), ())), preferred_element_type=f32)


def matmul_tn(left, right):
    return lax.dot_general(left, right, (((0,), (0,)), ((), ())), preferred_element_type=f32)


def angles(positions):
    inverse_freq = rope_base ** (-jnp.arange(0, HD // 2, dtype=f32) * 2.0 / HD)
    phase = positions[:, None] * inverse_freq[None, :]
    cosine, sine = jnp.cos(phase), jnp.sin(phase)
    return jnp.concatenate([cosine, cosine], -1), jnp.concatenate([-sine, sine], -1)


def norm_back(upstream, normed, inv_rms, gain_row):
    scaled = upstream * gain_row
    return inv_rms * (scaled - normed * jnp.mean(scaled * normed, axis=-1, keepdims=True))


def rms_scale(values):
    return lax.rsqrt(jnp.mean(values * values, axis=-1, keepdims=True) + epsilon)


def local(
    residual,
    out_grad,
    lengths,
    attn_gain,
    query_weight,
    query_bias,
    key_weight,
    key_bias,
    value_weight,
    value_bias,
    output_weight,
    ffn_gain,
    gate_weight,
    up_weight,
    down_weight,
):
    rows, own, width = residual.shape
    tokens = rows * own
    shard = own * lax.axis_size("heads")
    n_heads = lax.axis_size("heads")
    n_seq = lax.axis_size("seq")
    z = lax.axis_index("heads")
    s = lax.axis_index("seq")
    c = lax.axis_index("dp")
    piece = c * n_seq + s
    order_a, order_b = seq_masks()
    both = ("dp", "seq")
    depth = gate_weight.shape[0]
    half = n_seq * depth
    q_own = query_weight.shape[1]
    q_all = q_own * n_heads
    kv_width = key_weight.shape[1]
    group_heads = H // KVH

    start = s * shard + z * own
    positions = start + jnp.arange(own, dtype=jnp.int32)
    cosine, sine = angles(positions.astype(f32))

    first_input, kv_own = first_call(
        residual, attn_gain, key_weight, value_weight, key_bias, value_bias, cosine, sine
    )
    kv_ring = gather_ring(kv_own, "heads")
    key_block = jnp.concatenate([part[..., :kv_width] for part in kv_ring], axis=1)
    value_block = jnp.concatenate([part[..., kv_width:] for part in kv_ring], axis=1)
    keys = jnp.concatenate(gather_seq(key_block, order_a, 1), axis=1)
    values = jnp.concatenate(gather_seq(value_block, order_b, 1), axis=1)
    seq_at = jnp.arange(n_seq, dtype=jnp.int32) ^ s
    ring_at = (jnp.arange(n_heads, dtype=jnp.int32) + z) % n_heads
    key_pos = (
        seq_at[:, None, None] * shard
        + ring_at[None, :, None] * own
        + jnp.arange(own, dtype=jnp.int32)[None, None, :]
    ).reshape(-1, 1)
    limit = jnp.minimum(positions[None, :], lengths[:, None] - 1)
    limit = jnp.tile(limit, (1, group_heads))[:, None, :]

    query_piece = take(query_weight, piece, depth, 0)
    output_piece = take(output_weight, piece, depth, 1).T
    extra = 16
    bias_rows = jnp.pad(query_bias[None], ((0, extra - 1), (0, q_own)))
    sent = jnp.concatenate(
        [jnp.concatenate([query_piece, output_piece], axis=1), bias_rows], axis=0
    )
    qo_ring = gather_ring(sent, "heads")
    back = (n_heads - z) % n_heads

    def in_order(pieces):
        return lax.dynamic_slice_in_dim(
            jnp.concatenate(pieces + pieces[:-1], axis=1), back * q_own, q_all, 1
        )

    query_rows = in_order([part[:depth, :q_own] for part in qo_ring])
    output_rows = in_order([part[:depth, q_own:] for part in qo_ring])
    bias_all = in_order([part[depth : depth + 1, :q_own] for part in qo_ring]).astype(f32)

    def gather_rows(block, masks):
        held = jnp.zeros((half, block.shape[1]), block.dtype)
        for r, part in enumerate(gather_seq(block, masks, 0)):
            held = lax.dynamic_update_slice_in_dim(held, part, (s ^ r) * depth, 0)
        other = swap(held, "dp", 1)
        full = jnp.zeros((2 * half, block.shape[1]), block.dtype)
        full = lax.dynamic_update_slice_in_dim(full, held, c * half, 0)
        return lax.dynamic_update_slice_in_dim(full, other, (1 - c) * half, 0)

    query_full = gather_rows(query_rows, order_a)
    output_full = gather_rows(output_rows, order_b)

    down_full = lax.all_gather(down_weight.T, both, axis=0, tiled=True)
    gate_full = lax.all_gather(gate_weight, both, axis=0, tiled=True)
    up_full = lax.all_gather(up_weight, both, axis=0, tiled=True)

    input_flat = first_input.reshape(tokens, width)
    query_lin = (matmul(input_flat, query_full) + bias_all).reshape(rows, own, q_all)
    attended, query_rot, logs = attend_call(
        query_lin, cosine, sine, keys, values, key_pos, limit
    )
    attended = attended.reshape(tokens, q_all)
    stream = residual.astype(f32).reshape(tokens, width)
    second_stream = stream + matmul_nt(attended, output_full)
    second_scale = rms_scale(second_stream)
    second_normed = second_stream * second_scale
    second_gain = ffn_gain.astype(f32)
    second_own = (second_normed * second_gain).astype(bf16).reshape(rows, own, width)

    count = rows * shard
    second_input = lax.all_gather(second_own, "heads", axis=1, tiled=True).reshape(count, width)
    grad_flat = out_grad.reshape(count, width)
    grad_hidden = matmul(grad_flat, down_full)
    gate_act = matmul(second_input, gate_full)
    up_act = matmul(second_input, up_full)
    sigmoid_gate = jax.nn.sigmoid(gate_act)
    silu_gate = gate_act * sigmoid_gate
    hidden = (silu_gate * up_act).astype(bf16)
    grad_gate = (
        grad_hidden * up_act * sigmoid_gate * (1.0 + gate_act * (1.0 - sigmoid_gate))
    ).astype(bf16)
    grad_up = (grad_hidden * silu_gate).astype(bf16)
    second_back = matmul_nt(grad_gate, gate_full) + matmul_nt(grad_up, up_full)
    second_back = lax.psum_scatter(
        second_back.astype(bf16).reshape(rows, shard, width),
        "heads",
        scatter_dimension=1,
        tiled=True,
    )
    ffn_part = matmul_nt(hidden, down_full).astype(bf16).reshape(rows, shard, width)
    ffn_own = lax.psum_scatter(ffn_part, "heads", scatter_dimension=1, tiled=True)
    block_out = second_stream.reshape(rows, own, width) + ffn_own.astype(f32)
    down_grad = matmul_tn(grad_flat, hidden).astype(bf16)
    gate_grad = matmul_tn(second_input, grad_gate).astype(bf16)
    up_grad = matmul_tn(second_input, grad_up).astype(bf16)
    down_grad, gate_grad, up_grad = (
        lax.psum_scatter(item, both, scatter_dimension=0, tiled=True).astype(f32)
        for item in (down_grad, gate_grad, up_grad)
    )

    second_back = second_back.reshape(tokens, width).astype(f32)
    second_gain_term = jnp.sum(second_back * second_normed, axis=0)
    grad_own = take(out_grad, z, own, 1).reshape(tokens, width).astype(f32)
    grad_stream = grad_own + norm_back(second_back, second_normed, second_scale, second_gain)
    grad_attn = grad_stream.astype(bf16)

    grad_attended = matmul(grad_attn, output_full).astype(bf16)
    grad_query, key_terms, value_terms = attend_back_call(
        query_rot,
        grad_attended.reshape(rows, own, q_all),
        cosine,
        sine,
        keys,
        values,
        key_pos,
        limit,
        logs,
    )
    key_terms = scatter_seq(split(key_terms, n_seq, 1), order_b, 1)
    value_terms = scatter_seq(split(value_terms, n_seq, 1), order_a, 1)
    kv_terms = [
        jnp.concatenate(pair, axis=-1)
        for pair in zip(split(key_terms, n_heads, 1), split(value_terms, n_heads, 1))
    ]
    grad_kv = turn_back_call(scatter_ring(kv_terms, "heads"), cosine, sine)
    grad_kv = grad_kv.reshape(tokens, 2 * kv_width)
    grad_query = grad_query.reshape(tokens, q_all)

    query_grad = matmul_tn(input_flat, grad_query).astype(bf16)
    output_grad = matmul_tn(grad_attn, attended).astype(bf16)

    def scatter_rows(full, masks):
        mine = add_low(take(full, c, half, 0), swap(take(full, 1 - c, half, 0), "dp", 1))
        blocks = [take(mine, s ^ r, depth, 0) for r in range(n_seq)]
        return scatter_seq(blocks, masks, 0)

    query_part = scatter_rows(query_grad, order_b)
    output_part = scatter_rows(output_grad, order_a)
    qo_parts = [
        jnp.concatenate(
            [
                take(part, (z + m) % n_heads, q_own, 1)
                for part in (query_part, output_part)
            ],
            axis=1,
        )
        for m in range(n_heads)
    ]
    qo_grad = scatter_ring(qo_parts, "heads").astype(f32)
    query_weight_grad = qo_grad[:, :q_own]
    output_weight_grad = qo_grad[:, q_own:].T

    kv_grad = matmul_tn(input_flat, grad_kv).astype(bf16)
    kv_part = scatter_rows(kv_grad, order_a)
    kv_cut = kv_width // n_heads
    kv_parts = [
        jnp.concatenate(
            [
                take(part, (z + m) % n_heads, kv_cut, 1)
                for part in (kv_part[:, :kv_width], kv_part[:, kv_width:])
            ],
            axis=1,
        )
        for m in range(n_heads)
    ]
    kv_sum = scatter_ring(kv_parts, "heads").astype(f32)

    first_scale = rms_scale(stream)
    first_normed = stream * first_scale
    first_gain = attn_gain.astype(f32)
    first_back = (
        matmul_nt(grad_query, query_full)
        + matmul_nt(grad_kv[:, :kv_width], key_weight)
        + matmul_nt(grad_kv[:, kv_width:], value_weight)
    )
    first_gain_term = jnp.sum(first_back * first_normed, axis=0)
    residual_grad = grad_stream + norm_back(first_back, first_normed, first_scale, first_gain)

    terms = [
        first_gain_term,
        second_gain_term,
        jnp.sum(grad_query.astype(f32), axis=0),
        jnp.sum(grad_kv.astype(f32), axis=0),
    ]
    sums = jnp.concatenate(terms).reshape(-1, HD)
    for axis in ("dp", "seq", "heads"):
        bit = 1
        while bit < lax.axis_size(axis):
            sums = sums + swap(sums, axis, bit)
            bit *= 2
    sums = sums.reshape(-1)
    gain_piece = width // (lax.axis_size("dp") * n_seq * n_heads)
    gain_at = (piece * n_heads + z) * gain_piece
    attn_gain_grad = lax.dynamic_slice_in_dim(sums, gain_at, gain_piece, 0)
    ffn_gain_grad = lax.dynamic_slice_in_dim(sums, width + gain_at, gain_piece, 0)
    query_bias_grad = lax.dynamic_slice_in_dim(sums, 2 * width + z * q_own, q_own, 0)
    kv_at = 2 * width + q_all + z * kv_cut
    key_bias_grad = lax.dynamic_slice_in_dim(sums, kv_at, kv_cut, 0)
    value_bias_grad = lax.dynamic_slice_in_dim(sums, kv_at + kv_width, kv_cut, 0)

    return (
        block_out.astype(bf16),
        residual_grad.reshape(rows, own, width),
        attn_gain_grad,
        query_weight_grad,
        query_bias_grad,
        kv_sum[:, :kv_cut],
        key_bias_grad,
        kv_sum[:, kv_cut:],
        value_bias_grad,
        output_weight_grad,
        ffn_gain_grad,
        gate_grad,
        up_grad,
        down_grad.T,
    )


def solution(mesh):
    in_specs = (
        P("dp", ("seq", "heads"), None),
        P("dp", "seq", None),
        P("dp"),
        P(),
        P(None, "heads"),
        P("heads"),
        P(),
        P(),
        P(),
        P(),
        P("heads", None),
        P(),
        P(("dp", "seq"), "heads"),
        P(("dp", "seq"), "heads"),
        P("heads", ("dp", "seq")),
    )
    out_specs = (
        P("dp", ("seq", "heads"), None),
        P("dp", ("seq", "heads"), None),
        P(("dp", "seq", "heads")),
        P(("dp", "seq"), "heads"),
        P("heads"),
        P(("dp", "seq"), "heads"),
        P("heads"),
        P(("dp", "seq"), "heads"),
        P("heads"),
        P("heads", ("dp", "seq")),
        P(("dp", "seq", "heads")),
        P(("dp", "seq"), "heads"),
        P(("dp", "seq"), "heads"),
        P("heads", ("dp", "seq")),
    )
    return jax.shard_map(local, mesh=mesh, in_specs=in_specs, out_specs=out_specs, check_vma=False)
```

```python
import jax
import jax.numpy as jnp
from jax import lax
from jax.experimental import pallas as pl
from jax.experimental.layout import Layout, with_layout_constraint
from jax.experimental.pallas import tpu as pltpu
from jax.sharding import PartitionSpec as P

H = 12
KVH = 2
HD = 128

epsilon = 1e-06
rope_base = 1000000.0
hidden_logit = -1e30
log2_e = 1.4426950408889634

bf16 = jnp.bfloat16
f32 = jnp.float32
vmem_bytes = 48 * 2**20


def after(value, earlier):
    return lax.optimization_barrier((value, earlier))[0]


def swap(value, axis, mask):
    pairs = [(source, source ^ mask) for source in range(lax.axis_size(axis))]
    return lax.ppermute(value, axis, pairs)


def rotate_down(value, axis):
    size = lax.axis_size(axis)
    pairs = [(source, (source - 1) % size) for source in range(size)]
    return lax.ppermute(value, axis, pairs)


class Lanes:
    def __init__(self):
        self.sent = {}
        self.came = {}

    def send(self, key, value, move):
        sent, came = self.sent.setdefault(key, []), self.came.setdefault(key, [])
        if sent:
            value = after(value, (sent[-1], came[-2:][0]) if len(came) > 1 else sent[-1])
        sent.append(value)
        came.append(move(value))
        return came[-1]

    def seq(self, value, stage):
        size = lax.axis_size("seq")
        pairs = [
            (core * size + place, core * size + (place ^ masks[stage]))
            for core, masks in enumerate(seq_masks())
            for place in range(size)
        ]
        return self.send("seq", value, lambda v: lax.ppermute(v, ("dp", "seq"), pairs))

    def core(self, value):
        return self.send("dp", value, lambda v: swap(v, "dp", 1))

    def direct(self, values, away, gate=None):
        size = lax.axis_size("heads")
        if gate is not None:
            values = after(values, gate)
        return [
            lax.ppermute(
                value, "heads", [(i, (i + m if away else i - m) % size) for i in range(size)]
            )
            for m, value in enumerate(values, 1)
        ]

    def gather(self, block, gate=None):
        return [block] + self.direct([block] * (lax.axis_size("heads") - 1), False, gate)

    def ring(self, value):
        return self.send("heads", value, lambda v: rotate_down(v, "heads"))


class Order:
    def __init__(self):
        self.last = None

    def then(self, value):
        return value if self.last is None else after(value, self.last)

    def mark(self, value):
        self.last = value
        return value


def total_of(parts):
    result = parts[0].astype(f32)
    for part in parts[1:]:
        result = result + part.astype(f32)
    return result


def low_total(parts):
    return parts[0] if len(parts) == 1 else total_of(parts).astype(bf16)


def as_sent(sums):
    return lax.reduce_precision(sums, exponent_bits=8, mantissa_bits=7)


def join(parts, dim):
    return parts[0] if len(parts) == 1 else jnp.concatenate(parts, axis=dim)


def split(value, count, dim):
    return [value] if count == 1 else jnp.split(value, count, axis=dim)


def seq_masks():
    bits = lax.axis_size("seq").bit_length() - 1
    masks = [1 << bit for bit in range(bits)]
    return masks, masks[bits // 2 :] + masks[: bits // 2]


def seq_places():
    at = []
    for masks in seq_masks():
        mixed = [0]
        for mask in masks:
            mixed += [m ^ mask for m in mixed]
        at.append(mixed)
    s, c = lax.axis_index("seq"), lax.axis_index("dp")
    return [s ^ jnp.where(c == 0, first, second) for first, second in zip(*at)]


class SeqGather:
    def __init__(self, lanes, block, dim):
        self.lanes, self.held, self.dim, self.stage = lanes, [block], dim, 0

    def step(self):
        came = self.lanes.seq(join(self.held, self.dim), self.stage)
        self.held = self.held + [came]
        self.stage += 1
        return self

    def blocks(self, gate):
        parts, count = [], 1
        for index, part in enumerate(after(self.held, gate)):
            parts += split(part, count, self.dim)
            count *= 2 if index else 1
        return parts


class SeqScatter:
    def __init__(self, lanes, items, dim):
        self.lanes, self.items, self.dim = lanes, items, dim

    def step(self, message=None):
        half = len(self.items[0]) // 2
        if message is None:
            message = join(
                [low_total(terms) for held in self.items for terms in held[half:]], self.dim
            )
        came = self.lanes.seq(message, half.bit_length() - 1)
        parts = split(came, half * len(self.items), self.dim)
        self.items = [
            [terms + [parts[i * half + p]] for p, terms in enumerate(held[:half])]
            for i, held in enumerate(self.items)
        ]
        return self

    def terms(self):
        while len(self.items[0]) > 1:
            self.step()
        return [held[0] for held in self.items]


def gather_ring(lanes, block):
    held = [block]
    for _ in range(lax.axis_size("heads") - 1):
        held.append(lanes.ring(held[-1]))
    return held


def scatter_ring(lanes, blocks):
    terms = blocks[1]
    for block in blocks[2:] + blocks[:1]:
        terms = [lanes.ring(low_total(terms))] + block
    return terms


def by_rows(value):
    return with_layout_constraint(value, Layout(major_to_minor=tuple(range(value.ndim))))


def take(value, index, size, dim):
    return lax.dynamic_slice_in_dim(value, index * size, size, dim)


def turn(values, cosine, sine):
    return values * cosine + pltpu.roll(values, HD // 2, 1) * sine


def turn_back(values, cosine, sine):
    return values * cosine - pltpu.roll(values, HD // 2, 1) * sine


def first_kernel(x_ref, gain_ref, kw_ref, vw_ref, kb_ref, vb_ref, cos_ref, sin_ref, in_ref, kv_ref):
    x = x_ref[0].astype(f32)
    scale = lax.rsqrt(jnp.mean(x * x, axis=-1, keepdims=True) + epsilon)
    low = (x * scale * gain_ref[...].astype(f32)).astype(bf16)
    in_ref[0] = low
    width = kw_ref.shape[1]
    keys = jnp.dot(low, kw_ref[...], preferred_element_type=f32) + kb_ref[...].astype(f32)
    for at in range(0, width, HD):
        kv_ref[0, :, at : at + HD] = turn(
            keys[:, at : at + HD], cos_ref[...], sin_ref[...]
        ).astype(bf16)
    values = jnp.dot(low, vw_ref[...], preferred_element_type=f32) + vb_ref[...].astype(f32)
    kv_ref[0, :, width:] = values.astype(bf16)


def first_call(residual, gain, kw, vw, kb, vb, cosine, sine):
    rows, count, width = residual.shape
    kv = kw.shape[1]
    fixed = lambda shape: pl.BlockSpec(shape, lambda r: (0, 0))
    row = lambda size: pl.BlockSpec((1, count, size), lambda r: (r, 0, 0))
    return pl.pallas_call(
        first_kernel,
        grid=(rows,),
        in_specs=[
            row(width),
            fixed((1, width)),
            fixed((width, kv)),
            fixed((width, kv)),
            fixed((1, kv)),
            fixed((1, kv)),
            fixed((count, HD)),
            fixed((count, HD)),
        ],
        out_specs=[row(width), row(2 * kv)],
        out_shape=[
            jax.ShapeDtypeStruct((rows, count, width), bf16),
            jax.ShapeDtypeStruct((rows, count, 2 * kv), bf16),
        ],
        cost_estimate=pl.CostEstimate(
            flops=4 * rows * count * width * kv,
            bytes_accessed=2 * (2 * rows * count * width + 2 * width * kv),
            transcendentals=0,
        ),
        compiler_params=pltpu.CompilerParams(vmem_limit_bytes=vmem_bytes),
        name="first_norm",
    )(residual, gain[None], kw, vw, kb[None], vb[None], cosine, sine)


def head_columns(shift_ref, width):
    heads = width // HD
    first = pl.program_id(1) * (heads // KVH) + shift_ref[0]
    places = [lax.rem(first + h, heads) for h in range(heads // KVH)]
    return [pl.ds(pl.multiple_of(place * HD, HD), HD) for place in places]


def attend_kernel(
    shift_ref,
    q_ref,
    cos_ref,
    sin_ref,
    k_ref,
    v_ref,
    kpos_ref,
    limit_ref,
    out_ref,
    turned_ref,
    log_ref,
):
    count = q_ref.shape[1]
    columns = head_columns(shift_ref, q_ref.shape[2])
    turned = []
    for at in columns:
        u = turn(q_ref[0, :, at], cos_ref[...], sin_ref[...])
        turned_ref[0, :, at] = u.astype(bf16)
        turned.append(u)
    query = jnp.concatenate(turned, axis=0).astype(bf16)
    scores = lax.dot_general(
        k_ref[0], query, (((1,), (1,)), ((), ())), preferred_element_type=f32
    )
    seen = kpos_ref[...] <= limit_ref[0]
    scores = jnp.where(seen, scores * (HD**-0.5 * log2_e), hidden_logit)
    peak = jnp.max(scores, axis=0, keepdims=True)
    weight = jnp.exp2(scores - peak)
    total = jnp.sum(weight, axis=0, keepdims=True)
    log_ref[0, 0] = peak + jnp.log2(total)
    out = lax.dot_general(
        v_ref[0], weight.astype(bf16), (((0,), (0,)), ((), ())), preferred_element_type=f32
    )
    out = (out * (1.0 / total)).T
    for h, at in enumerate(columns):
        out_ref[0, :, at] = out[h * count : (h + 1) * count].astype(bf16)


def attend_call(shift, query, cosine, sine, kv, kpos, limit):
    rows, count, width = query.shape
    length = kv.shape[1]
    groups = KVH
    many = limit.shape[2]
    part = pl.BlockSpec((1, count, width), lambda r, g, shift: (r, 0, 0))
    fixed = lambda shape: pl.BlockSpec(shape, lambda r, g, shift: (0, 0))
    keys = pl.BlockSpec((1, length, HD), lambda r, g, shift: (r, 0, g))
    values = pl.BlockSpec((1, length, HD), lambda r, g, shift: (r, 0, KVH + g))
    work = rows * groups * length * many
    return pl.pallas_call(
        attend_kernel,
        grid_spec=pltpu.PrefetchScalarGridSpec(
            num_scalar_prefetch=1,
            grid=(rows, groups),
            in_specs=[
                part,
                fixed((count, HD)),
                fixed((count, HD)),
                keys,
                values,
                fixed((length, 1)),
                pl.BlockSpec((1, 1, many), lambda r, g, shift: (r, 0, 0)),
            ],
            out_specs=[part, part, pl.BlockSpec((1, 1, 1, many), lambda r, g, shift: (r, g, 0, 0))],
        ),
        out_shape=[
            jax.ShapeDtypeStruct((rows, count, width), bf16),
            jax.ShapeDtypeStruct((rows, count, width), bf16),
            jax.ShapeDtypeStruct((rows, groups, 1, many), f32),
        ],
        cost_estimate=pl.CostEstimate(
            flops=4 * work * HD, bytes_accessed=2 * kv.size, transcendentals=work
        ),
        compiler_params=pltpu.CompilerParams(vmem_limit_bytes=vmem_bytes),
        name="attend",
    )(shift, query, cosine, sine, kv, kv, kpos, limit)


def attend_back_kernel(
    shift_ref,
    q_ref,
    og_ref,
    cos_ref,
    sin_ref,
    k_ref,
    v_ref,
    kpos_ref,
    limit_ref,
    log_ref,
    gq_ref,
    low_ref,
    high_ref,
):
    count = q_ref.shape[1]
    columns = head_columns(shift_ref, q_ref.shape[2])

    def rows_of(ref):
        parts = [ref[0, :, at].astype(f32) for at in columns]
        return jnp.concatenate(parts, axis=0).astype(bf16)

    query, upstream = rows_of(q_ref), rows_of(og_ref)
    last = (((1,), (1,)), ((), ()))
    scores = lax.dot_general(k_ref[0], query, last, preferred_element_type=f32)
    seen = kpos_ref[...] <= limit_ref[0]
    scale = HD**-0.5
    probs = jnp.exp2(jnp.where(seen, scores * (scale * log2_e) - log_ref[0, 0], hidden_logit))
    at_keys, at_values = (
        pl.ds(pl.multiple_of((first + pl.program_id(1)) * HD, HD), HD) for first in (0, KVH)
    )
    middle = low_ref.shape[1]
    grad_values = jnp.dot(probs.astype(bf16), upstream, preferred_element_type=f32)
    low_ref[0, :, at_values] = grad_values[:middle].astype(bf16)
    high_ref[0, :, at_values] = grad_values[middle:].astype(bf16)
    grad_probs = lax.dot_general(v_ref[0], upstream, last, preferred_element_type=f32)
    mixed = probs * grad_probs
    total = jnp.sum(mixed, axis=0, keepdims=True)
    grad_scores = ((mixed - probs * total) * scale).astype(bf16)
    grad_keys = jnp.dot(grad_scores, query, preferred_element_type=f32)
    low_ref[0, :, at_keys] = grad_keys[:middle].astype(bf16)
    high_ref[0, :, at_keys] = grad_keys[middle:].astype(bf16)
    grad_query = lax.dot_general(
        k_ref[0], grad_scores, (((0,), (0,)), ((), ())), preferred_element_type=f32
    ).T
    for h, at in enumerate(columns):
        gq_ref[0, :, at] = turn_back(
            grad_query[h * count : (h + 1) * count], cos_ref[...], sin_ref[...]
        ).astype(bf16)


def attend_back_call(shift, query, upstream, cosine, sine, kv, kpos, limit, logs):
    rows, count, width = query.shape
    length = kv.shape[1]
    groups = KVH
    many = limit.shape[2]
    part = pl.BlockSpec((1, count, width), lambda r, g, shift: (r, 0, 0))
    fixed = lambda shape: pl.BlockSpec(shape, lambda r, g, shift: (0, 0))
    keys = pl.BlockSpec((1, length, HD), lambda r, g, shift: (r, 0, g))
    values = pl.BlockSpec((1, length, HD), lambda r, g, shift: (r, 0, KVH + g))
    work = rows * groups * length * many
    return pl.pallas_call(
        attend_back_kernel,
        grid_spec=pltpu.PrefetchScalarGridSpec(
            num_scalar_prefetch=1,
            grid=(rows, groups),
            in_specs=[
                part,
                part,
                fixed((count, HD)),
                fixed((count, HD)),
                keys,
                values,
                fixed((length, 1)),
                pl.BlockSpec((1, 1, many), lambda r, g, shift: (r, 0, 0)),
                pl.BlockSpec((1, 1, 1, many), lambda r, g, shift: (r, g, 0, 0)),
            ],
            out_specs=[
                part,
                pl.BlockSpec((1, length // 2, 2 * KVH * HD), lambda r, g, shift: (r, 0, 0)),
                pl.BlockSpec((1, length // 2, 2 * KVH * HD), lambda r, g, shift: (r, 0, 0)),
            ],
        ),
        out_shape=[
            jax.ShapeDtypeStruct((rows, count, width), bf16),
            jax.ShapeDtypeStruct((rows, length // 2, 2 * KVH * HD), bf16),
            jax.ShapeDtypeStruct((rows, length // 2, 2 * KVH * HD), bf16),
        ],
        cost_estimate=pl.CostEstimate(
            flops=10 * work * HD, bytes_accessed=4 * kv.size, transcendentals=work
        ),
        compiler_params=pltpu.CompilerParams(vmem_limit_bytes=vmem_bytes),
        name="attend_back",
    )(shift, query, upstream, cosine, sine, kv, kv, kpos, limit, logs)


def turn_back_kernel(kv_ref, cos_ref, sin_ref, out_ref):
    half = kv_ref.shape[2] // 2
    for at in range(0, half, HD):
        out_ref[0, :, at : at + HD] = turn_back(
            kv_ref[0, :, at : at + HD].astype(f32), cos_ref[...], sin_ref[...]
        ).astype(bf16)
    out_ref[0, :, half:] = kv_ref[0, :, half:]


def turn_back_call(kv, cosine, sine):
    rows, count, width = kv.shape
    row = pl.BlockSpec((1, count, width), lambda r: (r, 0, 0))
    table = pl.BlockSpec((count, HD), lambda r: (0, 0))
    return pl.pallas_call(
        turn_back_kernel,
        grid=(rows,),
        in_specs=[row, table, table],
        out_specs=row,
        out_shape=jax.ShapeDtypeStruct(kv.shape, bf16),
        cost_estimate=pl.CostEstimate(
            flops=4 * kv.size, bytes_accessed=4 * kv.size, transcendentals=0
        ),
        compiler_params=pltpu.CompilerParams(vmem_limit_bytes=vmem_bytes),
        name="turn_back",
    )(kv, cosine, sine)


def matmul(left, right):
    return jnp.dot(left, right, preferred_element_type=f32)


def matmul_nt(left, right):
    return lax.dot_general(left, right, (((1,), (1,)), ((), ())), preferred_element_type=f32)


def matmul_tn(left, right):
    return lax.dot_general(left, right, (((0,), (0,)), ((), ())), preferred_element_type=f32)


def angles(positions):
    inverse_freq = rope_base ** (-jnp.arange(0, HD // 2, dtype=f32) * 2.0 / HD)
    phase = positions[:, None] * inverse_freq[None, :]
    cosine, sine = jnp.cos(phase), jnp.sin(phase)
    return jnp.concatenate([cosine, cosine], -1), jnp.concatenate([-sine, sine], -1)


def norm_back(upstream, normed, inv_rms, gain_row):
    scaled = upstream * gain_row
    return inv_rms * (scaled - normed * jnp.mean(scaled * normed, axis=-1, keepdims=True))


def rms_scale(values):
    return lax.rsqrt(jnp.mean(values * values, axis=-1, keepdims=True) + epsilon)


def local(
    residual,
    out_grad,
    lengths,
    attn_gain,
    query_weight,
    query_bias,
    key_weight,
    key_bias,
    value_weight,
    value_bias,
    output_weight,
    ffn_gain,
    gate_weight,
    up_weight,
    down_weight,
):
    rows, own, width = residual.shape
    tokens = rows * own
    shard = own * lax.axis_size("heads")
    n_heads = lax.axis_size("heads")
    n_seq = lax.axis_size("seq")
    z = lax.axis_index("heads")
    s = lax.axis_index("seq")
    c = lax.axis_index("dp")
    piece = c * n_seq + s
    order_a, order_b = seq_masks()
    depth = gate_weight.shape[0]
    half = n_seq * depth
    q_own = query_weight.shape[1]
    q_all = q_own * n_heads
    kv_width = key_weight.shape[1]
    group_heads = H // KVH

    start = s * shard + z * own
    positions = start + jnp.arange(own, dtype=jnp.int32)
    cosine, sine = angles(positions.astype(f32))

    lanes = Lanes()
    places = seq_places()
    stages = range(len(places).bit_length() - 1)

    def both_cores(mine):
        other = lanes.core(mine)
        full = jnp.zeros((2 * half, mine.shape[1]), bf16)
        full = lax.dynamic_update_slice_in_dim(full, mine, c * half, 0)
        return by_rows(lax.dynamic_update_slice_in_dim(full, other, (1 - c) * half, 0))

    def halves_grad(left, right):
        terms = [
            order.mark(by_rows(matmul_tn(take(left, at, half, 1), order.then(right)).astype(bf16)))
            for at in (1 - c, c)
        ]
        return [terms[1], lanes.core(terms[0])]

    def row_blocks(parts):
        return [[take(part, place, depth, 0) for part in parts] for place in places]

    units = gate_weight.shape[1]
    spare = -units % 256
    both = ("dp", "seq")
    down_full, gate_full, up_full = (
        lax.all_gather(jnp.pad(part, ((0, 0), (0, spare))), both, axis=0, tiled=True)
        for part in (down_weight.T, gate_weight, up_weight)
    )

    first_input, kv_own = first_call(
        residual, attn_gain, key_weight, value_weight, key_bias, value_bias, cosine, sine
    )
    kv_ring = lanes.gather(kv_own)
    kv_gather = SeqGather(lanes, jnp.concatenate(kv_ring, axis=1), 1)
    for _ in stages:
        kv_gather.step()
    kv_sent = lanes.sent["seq"][-1]
    kv_all = jnp.concatenate(kv_gather.held, axis=1)
    ring_at = (jnp.arange(n_heads, dtype=jnp.int32) + z) % n_heads
    key_pos = (
        jnp.stack(places)[:, None, None] * shard
        + ring_at[None, :, None] * own
        + jnp.arange(own, dtype=jnp.int32)[None, None, :]
    ).reshape(-1, 1)
    limit = jnp.minimum(positions[None, :], lengths[:, None] - 1)
    limit = jnp.tile(limit, (1, group_heads))[:, None, :]

    extra = 16
    query_half = take(query_weight, c, half, 0)
    bias_rows = jnp.pad(query_bias[None], ((0, extra - 1), (0, 0)))
    query_ring = lanes.gather(jnp.concatenate([query_half, bias_rows], axis=0), kv_ring)
    bias_all = jnp.concatenate([part[half : half + 1] for part in query_ring], axis=1).astype(f32)
    query_rest = both_cores(
        jnp.concatenate([part[:half] for part in after(query_ring[1:], kv_sent)], axis=1)
    )
    output_ring = lanes.gather(take(output_weight, c, half, 1).T, query_ring)
    shift = ((H - z * (q_own // HD)) % H).reshape(1)

    input_flat = first_input.reshape(tokens, width)
    query_lin = jnp.concatenate(
        [matmul(input_flat, query_weight), matmul(input_flat, query_rest)], axis=1
    )
    query_lin = (query_lin + bias_all).reshape(rows, own, q_all)
    attended, query_rot, logs = attend_call(
        shift, query_lin, cosine, sine, kv_all, key_pos, limit
    )
    attended = attended.reshape(tokens, q_all)
    output_rest = both_cores(jnp.concatenate(after(output_ring[1:], attended), axis=1))
    stream = residual.astype(f32).reshape(tokens, width)
    second_stream = (
        stream
        + matmul(attended[:, :q_own], output_weight)
        + matmul_nt(attended[:, q_own:], output_rest)
    )
    second_scale = rms_scale(second_stream)
    second_normed = second_stream * second_scale
    second_gain = ffn_gain.astype(f32)
    second_own = (second_normed * second_gain).astype(bf16)

    order = Order()
    order.mark(second_own)
    tokens_ring = gather_ring(lanes, second_own)
    grad_flat = out_grad.reshape(rows, n_heads, own, width).transpose(1, 0, 2, 3)
    grad_flat = grad_flat.reshape(n_heads * tokens, width)
    grad_hidden_all = order.mark(matmul(order.then(grad_flat), down_full))

    def all_tokens(parts):
        full = jnp.zeros((n_heads * tokens, parts[0].shape[1]), bf16)
        for m, part in enumerate(parts):
            full = lax.dynamic_update_slice_in_dim(full, part, (z + m) % n_heads * tokens, 0)
        return by_rows(full)

    hidden_parts, gate_parts, up_parts, back_parts = [], [], [], []
    for m, part in enumerate(tokens_ring):
        part = order.then(part)
        grad_hidden = take(grad_hidden_all, (z + m) % n_heads, tokens, 0)
        gate_act = matmul(part, gate_full)
        up_act = matmul(part, up_full)
        sigmoid_gate = jax.nn.sigmoid(gate_act)
        silu_gate = gate_act * sigmoid_gate
        hidden_parts.append(by_rows((silu_gate * up_act).astype(bf16)))
        gate_parts.append(
            by_rows(
                (
                    grad_hidden * up_act * sigmoid_gate * (1.0 + gate_act * (1.0 - sigmoid_gate))
                ).astype(bf16)
            )
        )
        up_parts.append(by_rows((grad_hidden * silu_gate).astype(bf16)))
        back = matmul_nt(gate_parts[m], gate_full) + matmul_nt(up_parts[m], up_full)
        back_parts.append(order.mark(back.astype(bf16)))
    back_all = order.mark(all_tokens(back_parts))
    second_back = lax.psum_scatter(back_all, "heads", scatter_dimension=0, tiled=True)

    hidden = order.mark(all_tokens(order.then(hidden_parts)))
    down_terms = halves_grad(grad_flat, hidden)
    ffn_part = order.mark(matmul_nt(order.then(hidden), down_full).astype(bf16))
    ffn_own = lax.psum_scatter(
        after(ffn_part, back_all), "heads", scatter_dimension=0, tiled=True
    )
    block_out = (second_stream + ffn_own.astype(f32)).reshape(rows, own, width)
    second_input = order.mark(all_tokens(order.then(tokens_ring)))
    gate_terms = halves_grad(second_input, all_tokens(order.then(gate_parts)))
    down_scatter = SeqScatter(lanes, [row_blocks(order.then(down_terms))], 0).step()
    order.mark(lanes.sent["seq"][-1])
    up_terms = halves_grad(second_input, all_tokens(order.then(up_parts)))
    down_scatter.items = order.then(down_scatter.items)
    down_grad = total_of(down_scatter.terms()[0])[:, :units]
    order.mark(lanes.sent["seq"][-1])
    both_scatter = SeqScatter(
        lanes, order.then([row_blocks(gate_terms), row_blocks(up_terms)]), 0
    ).step()
    order.mark(lanes.sent["seq"][-1])

    second_back = order.then(second_back).astype(f32)
    second_gain_term = jnp.sum(second_back * second_normed, axis=0)
    grad_own = take(out_grad, z, own, 1).reshape(tokens, width).astype(f32)
    grad_stream = grad_own + norm_back(second_back, second_normed, second_scale, second_gain)
    grad_attn = grad_stream.astype(bf16)

    grad_attended = jnp.concatenate(
        [matmul_nt(grad_attn, output_weight), matmul(grad_attn, output_rest)], axis=1
    ).astype(bf16)
    grad_query, kv_low, kv_high = attend_back_call(
        shift,
        query_rot,
        grad_attended.reshape(rows, own, q_all),
        cosine,
        sine,
        kv_all,
        key_pos,
        limit,
        logs,
    )
    order.mark(grad_query)
    grad_query = grad_query.reshape(tokens, q_all)
    gate_sum, up_sum = both_scatter.terms()
    kv_scatter = SeqScatter(
        lanes,
        [[[part] for half_of in (kv_low, kv_high) for part in split(half_of, n_seq // 2, 1)]],
        1,
    ).step(kv_high)
    query_terms = halves_grad(input_flat, grad_query)
    output_terms = halves_grad(grad_attn, attended)
    kv_scatter.items = order.then(kv_scatter.items)
    (kv_terms,) = kv_scatter.terms()
    order.mark(lanes.sent["seq"][-1])
    gate_grad, up_grad = (total_of(order.then(terms))[:, :units] for terms in (gate_sum, up_sum))

    kv_sum = total_of(order.then(kv_terms)).astype(bf16)
    kv_away = order.mark(
        [take(kv_sum, m, own, 1) for m in range(1, n_heads)]
    )
    kv_came = lanes.direct(kv_away, True)

    qo_scatter = SeqScatter(
        lanes, order.then([row_blocks(query_terms), row_blocks(output_terms)]), 0
    ).step()
    order.mark(lanes.sent["seq"][-1])
    first_scale = rms_scale(stream)
    first_normed = stream * first_scale
    first_gain = attn_gain.astype(f32)
    first_back = order.mark(
        matmul_nt(order.then(grad_query[:, :q_own]), query_weight)
        + matmul_nt(order.then(grad_query[:, q_own:]), query_rest)
    )
    grad_kv = turn_back_call(
        total_of([take(kv_sum, 0, own, 1)] + order.then(kv_came)).astype(bf16), cosine, sine
    )
    grad_kv = order.mark(grad_kv.reshape(tokens, 2 * kv_width))

    first_back = (
        first_back
        + matmul_nt(grad_kv[:, :kv_width], key_weight)
        + matmul_nt(grad_kv[:, kv_width:], value_weight)
    )
    first_gain_term = jnp.sum(first_back * first_normed, axis=0)

    small = jnp.concatenate(
        [
            first_gain_term,
            second_gain_term,
            jnp.roll(jnp.sum(grad_query.astype(f32), axis=0), z * q_own),
            jnp.sum(grad_kv.astype(f32), axis=0),
        ]
    )
    kv_cut = kv_width // n_heads
    packed = 2 * kv_width
    lines = -(-small.size // (packed * 16)) * 16
    small = as_sent(jnp.pad(small, (0, lines * packed - small.size)).reshape(lines, packed))

    def with_small(value):
        return jnp.concatenate([value, small.astype(bf16)], axis=0)

    def apart(value):
        return value[:-lines], value[-lines:].astype(f32)

    kv_mine, kv_other = (
        matmul_tn(take(input_flat, at, half, 1), grad_kv).astype(bf16) for at in (c, 1 - c)
    )
    kv_other, came_small = apart(lanes.core(with_small(kv_other)))
    small = as_sent(small + came_small)
    kv_terms = row_blocks([kv_mine, kv_other])
    while len(kv_terms) > 1:
        count = len(kv_terms) // 2
        message = join([low_total(terms) for terms in kv_terms[count:]], 0)
        came, came_small = apart(lanes.seq(with_small(message), count.bit_length() - 1))
        small = as_sent(small + came_small)
        kv_terms = [terms + [came[p * depth : (p + 1) * depth]] for p, terms in enumerate(kv_terms[:count])]
    kv_part = low_total(kv_terms[0])
    low_small = small.astype(bf16).reshape(-1, 2 * kv_cut)
    kv_pieces = [
        jnp.concatenate(
            [
                take(part, (z + m) % n_heads, kv_cut, 1)
                for part in (kv_part[:, :kv_width], kv_part[:, kv_width:])
            ],
            axis=1,
        )
        for m in range(n_heads)
    ]
    came = lanes.direct(
        [jnp.concatenate([part, low_small], axis=0) for part in kv_pieces[1:]], True
    )
    kv_total = total_of([kv_pieces[0]] + [part[:depth] for part in came])
    sums = total_of([low_small] + [part[depth:] for part in came])
    sums = sums.reshape(-1)
    residual_grad = grad_stream + norm_back(first_back, first_normed, first_scale, first_gain)

    query_sum, output_sum = (low_total(terms) for terms in qo_scatter.terms())
    qo_parts = [
        jnp.concatenate(pair, axis=1)
        for pair in zip(split(query_sum, n_heads, 1), split(output_sum, n_heads, 1))
    ]
    qo_grad = total_of(qo_parts[:1] + lanes.direct(qo_parts[1:], True))
    query_weight_grad = qo_grad[:, :q_own]
    output_weight_grad = qo_grad[:, q_own:].T

    gain_piece = width // (lax.axis_size("dp") * n_seq * n_heads)
    gain_at = (piece * n_heads + z) * gain_piece
    attn_gain_grad = lax.dynamic_slice_in_dim(sums, gain_at, gain_piece, 0)
    ffn_gain_grad = lax.dynamic_slice_in_dim(sums, width + gain_at, gain_piece, 0)
    query_bias_grad = lax.dynamic_slice_in_dim(sums, 2 * width + z * q_own, q_own, 0)
    kv_at = 2 * width + q_all + z * kv_cut
    key_bias_grad = lax.dynamic_slice_in_dim(sums, kv_at, kv_cut, 0)
    value_bias_grad = lax.dynamic_slice_in_dim(sums, kv_at + kv_width, kv_cut, 0)

    return (
        block_out.astype(bf16),
        residual_grad.reshape(rows, own, width),
        attn_gain_grad,
        query_weight_grad,
        query_bias_grad,
        kv_total[:, :kv_cut],
        key_bias_grad,
        kv_total[:, kv_cut:],
        value_bias_grad,
        output_weight_grad,
        ffn_gain_grad,
        gate_grad,
        up_grad,
        down_grad.T,
    )


def solution(mesh):
    in_specs = (
        P("dp", ("seq", "heads"), None),
        P("dp", "seq", None),
        P("dp"),
        P(),
        P(None, "heads"),
        P("heads"),
        P(),
        P(),
        P(),
        P(),
        P("heads", None),
        P(),
        P(("dp", "seq"), "heads"),
        P(("dp", "seq"), "heads"),
        P("heads", ("dp", "seq")),
    )
    out_specs = (
        P("dp", ("seq", "heads"), None),
        P("dp", ("seq", "heads"), None),
        P(("dp", "seq", "heads")),
        P(("dp", "seq"), "heads"),
        P("heads"),
        P(("dp", "seq"), "heads"),
        P("heads"),
        P(("dp", "seq"), "heads"),
        P("heads"),
        P("heads", ("dp", "seq")),
        P(("dp", "seq", "heads")),
        P(("dp", "seq"), "heads"),
        P(("dp", "seq"), "heads"),
        P("heads", ("dp", "seq")),
    )
    return jax.shard_map(local, mesh=mesh, in_specs=in_specs, out_specs=out_specs, check_vma=False)
```

```python
import jax
import jax.numpy as jnp
from jax import lax
from jax.experimental import pallas as pl
from jax.experimental.layout import Layout, with_layout_constraint
from jax.experimental.pallas import tpu as pltpu
from jax.sharding import PartitionSpec as P

H = 12
KVH = 2
HD = 128

epsilon = 1e-06
rope_base = 1000000.0
hidden_logit = -1e30
log2_e = 1.4426950408889634

bf16 = jnp.bfloat16
f32 = jnp.float32
vmem_bytes = 48 * 2**20


def after(value, earlier):
    return lax.optimization_barrier((value, earlier))[0]


def tie(*values):
    return lax.optimization_barrier(values)


def swap(value, axis, mask):
    pairs = [(source, source ^ mask) for source in range(lax.axis_size(axis))]
    return lax.ppermute(value, axis, pairs)


def rotate_down(value, axis):
    size = lax.axis_size(axis)
    pairs = [(source, (source - 1) % size) for source in range(size)]
    return lax.ppermute(value, axis, pairs)


class Lanes:
    def __init__(self):
        self.sent = {}
        self.came = {}

    def send(self, key, value, move):
        sent, came = self.sent.setdefault(key, []), self.came.setdefault(key, [])
        if sent:
            value = after(value, (sent[-1], came[-2:][0]) if len(came) > 1 else sent[-1])
        sent.append(value)
        came.append(move(value))
        return came[-1]

    def seq(self, value, stage):
        size = lax.axis_size("seq")
        pairs = [
            (core * size + place, core * size + (place ^ masks[stage]))
            for core, masks in enumerate(seq_masks())
            for place in range(size)
        ]
        return self.send("seq", value, lambda v: lax.ppermute(v, ("dp", "seq"), pairs))

    def core(self, value):
        return self.send("dp", value, lambda v: swap(v, "dp", 1))

    def direct(self, values, away, gate=None):
        size = lax.axis_size("heads")
        if gate is not None:
            values = after(values, gate)
        return [
            lax.ppermute(
                value, "heads", [(i, (i + m if away else i - m) % size) for i in range(size)]
            )
            for m, value in enumerate(values, 1)
        ]

    def gather(self, block, gate=None):
        return [block] + self.direct([block] * (lax.axis_size("heads") - 1), False, gate)

    def ring(self, value):
        return self.send("heads", value, lambda v: rotate_down(v, "heads"))


class Order:
    def __init__(self):
        self.last = None

    def then(self, value):
        return value if self.last is None else after(value, self.last)

    def mark(self, value):
        self.last = value
        return value


def total_of(parts):
    result = parts[0].astype(f32)
    for part in parts[1:]:
        result = result + part.astype(f32)
    return result


def low_total(parts):
    return parts[0] if len(parts) == 1 else total_of(parts).astype(bf16)


def as_sent(sums):
    return lax.reduce_precision(sums, exponent_bits=8, mantissa_bits=7)


def join(parts, dim):
    return parts[0] if len(parts) == 1 else jnp.concatenate(parts, axis=dim)


def split(value, count, dim):
    return [value] if count == 1 else jnp.split(value, count, axis=dim)


def seq_masks():
    bits = lax.axis_size("seq").bit_length() - 1
    masks = [1 << bit for bit in range(bits)]
    return masks, masks[bits // 2 :] + masks[: bits // 2]


def seq_places():
    at = []
    for masks in seq_masks():
        mixed = [0]
        for mask in masks:
            mixed += [m ^ mask for m in mixed]
        at.append(mixed)
    s, c = lax.axis_index("seq"), lax.axis_index("dp")
    return [s ^ jnp.where(c == 0, first, second) for first, second in zip(*at)]


class SeqGather:
    def __init__(self, lanes, block, dim):
        self.lanes, self.held, self.dim, self.stage = lanes, [block], dim, 0

    def step(self):
        came = self.lanes.seq(join(self.held, self.dim), self.stage)
        self.held = self.held + [came]
        self.stage += 1
        return self

    def blocks(self, gate):
        parts, count = [], 1
        for index, part in enumerate(after(self.held, gate)):
            parts += split(part, count, self.dim)
            count *= 2 if index else 1
        return parts


class SeqScatter:
    def __init__(self, lanes, items, count, dim):
        self.lanes, self.items, self.count, self.dim = lanes, items, count, dim
        self.came = []

    def at(self, i, p):
        return self.items[i](p) + [came[i][p] for came in self.came]

    def step(self, message=None):
        half = self.count // 2
        each = range(len(self.items))
        if message is None:
            message = join(
                [low_total(self.at(i, p)) for i in each for p in range(half, self.count)],
                self.dim,
            )
        came = self.lanes.seq(message, half.bit_length() - 1)
        parts = split(came, half * len(self.items), self.dim)
        self.came.append([parts[i * half : (i + 1) * half] for i in each])
        self.count = half
        return self

    def terms(self):
        while self.count > 1:
            self.step()
        return [self.at(i, 0) for i in range(len(self.items))]


def by_rows(value):
    return with_layout_constraint(value, Layout(major_to_minor=tuple(range(value.ndim))))


def take(value, index, size, dim):
    return lax.dynamic_slice_in_dim(value, index * size, size, dim)


def turn(values, cosine, sine):
    return values * cosine + pltpu.roll(values, HD // 2, 1) * sine


def turn_back(values, cosine, sine):
    return values * cosine - pltpu.roll(values, HD // 2, 1) * sine


def first_kernel(x_ref, gain_ref, kw_ref, vw_ref, kb_ref, vb_ref, cos_ref, sin_ref, in_ref, kv_ref):
    x = x_ref[0].astype(f32)
    scale = lax.rsqrt(jnp.mean(x * x, axis=-1, keepdims=True) + epsilon)
    low = (x * scale * gain_ref[...].astype(f32)).astype(bf16)
    in_ref[0] = low
    width = kw_ref.shape[1]
    keys = jnp.dot(low, kw_ref[...], preferred_element_type=f32) + kb_ref[...].astype(f32)
    for at in range(0, width, HD):
        kv_ref[0, :, at : at + HD] = turn(
            keys[:, at : at + HD], cos_ref[...], sin_ref[...]
        ).astype(bf16)
    values = jnp.dot(low, vw_ref[...], preferred_element_type=f32) + vb_ref[...].astype(f32)
    kv_ref[0, :, width:] = values.astype(bf16)


def first_call(residual, gain, kw, vw, kb, vb, cosine, sine):
    rows, count, width = residual.shape
    kv = kw.shape[1]
    fixed = lambda shape: pl.BlockSpec(shape, lambda r: (0, 0))
    row = lambda size: pl.BlockSpec((1, count, size), lambda r: (r, 0, 0))
    return pl.pallas_call(
        first_kernel,
        grid=(rows,),
        in_specs=[
            row(width),
            fixed((1, width)),
            fixed((width, kv)),
            fixed((width, kv)),
            fixed((1, kv)),
            fixed((1, kv)),
            fixed((count, HD)),
            fixed((count, HD)),
        ],
        out_specs=[row(width), row(2 * kv)],
        out_shape=[
            jax.ShapeDtypeStruct((rows, count, width), bf16),
            jax.ShapeDtypeStruct((rows, count, 2 * kv), bf16),
        ],
        cost_estimate=pl.CostEstimate(
            flops=4 * rows * count * width * kv,
            bytes_accessed=2 * (2 * rows * count * width + 2 * width * kv),
            transcendentals=0,
        ),
        compiler_params=pltpu.CompilerParams(vmem_limit_bytes=vmem_bytes),
        name="first_norm",
    )(residual, gain[None], kw, vw, kb[None], vb[None], cosine, sine)


def head_columns(shift_ref, width):
    heads = width // HD
    first = pl.program_id(1) * (heads // KVH) + shift_ref[0]
    places = [lax.rem(first + h, heads) for h in range(heads // KVH)]
    return [pl.ds(pl.multiple_of(place * HD, HD), HD) for place in places]


def attend_kernel(
    shift_ref,
    q_ref,
    cos_ref,
    sin_ref,
    k_ref,
    v_ref,
    kpos_ref,
    limit_ref,
    out_ref,
    turned_ref,
    log_ref,
):
    count = q_ref.shape[1]
    columns = head_columns(shift_ref, q_ref.shape[2])
    turned = []
    for at in columns:
        u = turn(q_ref[0, :, at], cos_ref[...], sin_ref[...])
        turned_ref[0, :, at] = u.astype(bf16)
        turned.append(u)
    query = jnp.concatenate(turned, axis=0).astype(bf16)
    scores = lax.dot_general(
        k_ref[0], query, (((1,), (1,)), ((), ())), preferred_element_type=f32
    )
    seen = kpos_ref[...] <= limit_ref[0]
    scores = jnp.where(seen, scores * (HD**-0.5 * log2_e), hidden_logit)
    peak = jnp.max(scores, axis=0, keepdims=True)
    weight = jnp.exp2(scores - peak)
    total = jnp.sum(weight, axis=0, keepdims=True)
    log_ref[0, 0] = peak + jnp.log2(total)
    out = lax.dot_general(
        v_ref[0], weight.astype(bf16), (((0,), (0,)), ((), ())), preferred_element_type=f32
    )
    out = (out * (1.0 / total)).T
    for h, at in enumerate(columns):
        out_ref[0, :, at] = out[h * count : (h + 1) * count].astype(bf16)


def attend_call(shift, query, cosine, sine, kv, kpos, limit):
    rows, count, width = query.shape
    length = kv.shape[1]
    groups = KVH
    many = limit.shape[2]
    part = pl.BlockSpec((1, count, width), lambda r, g, shift: (r, 0, 0))
    fixed = lambda shape: pl.BlockSpec(shape, lambda r, g, shift: (0, 0))
    keys = pl.BlockSpec((1, length, HD), lambda r, g, shift: (r, 0, g))
    values = pl.BlockSpec((1, length, HD), lambda r, g, shift: (r, 0, KVH + g))
    work = rows * groups * length * many
    return pl.pallas_call(
        attend_kernel,
        grid_spec=pltpu.PrefetchScalarGridSpec(
            num_scalar_prefetch=1,
            grid=(rows, groups),
            in_specs=[
                part,
                fixed((count, HD)),
                fixed((count, HD)),
                keys,
                values,
                fixed((length, 1)),
                pl.BlockSpec((1, 1, many), lambda r, g, shift: (r, 0, 0)),
            ],
            out_specs=[part, part, pl.BlockSpec((1, 1, 1, many), lambda r, g, shift: (r, g, 0, 0))],
        ),
        out_shape=[
            jax.ShapeDtypeStruct((rows, count, width), bf16),
            jax.ShapeDtypeStruct((rows, count, width), bf16),
            jax.ShapeDtypeStruct((rows, groups, 1, many), f32),
        ],
        cost_estimate=pl.CostEstimate(
            flops=4 * work * HD, bytes_accessed=2 * kv.size, transcendentals=work
        ),
        compiler_params=pltpu.CompilerParams(vmem_limit_bytes=vmem_bytes),
        name="attend",
    )(shift, query, cosine, sine, kv, kv, kpos, limit)


def attend_back_kernel(
    shift_ref,
    q_ref,
    og_ref,
    cos_ref,
    sin_ref,
    k_ref,
    v_ref,
    kpos_ref,
    limit_ref,
    log_ref,
    gq_ref,
    low_ref,
    high_ref,
):
    count = q_ref.shape[1]
    columns = head_columns(shift_ref, q_ref.shape[2])

    def rows_of(ref):
        parts = [ref[0, :, at].astype(f32) for at in columns]
        return jnp.concatenate(parts, axis=0).astype(bf16)

    query, upstream = rows_of(q_ref), rows_of(og_ref)
    last = (((1,), (1,)), ((), ()))
    scores = lax.dot_general(k_ref[0], query, last, preferred_element_type=f32)
    seen = kpos_ref[...] <= limit_ref[0]
    scale = HD**-0.5
    probs = jnp.exp2(jnp.where(seen, scores * (scale * log2_e) - log_ref[0, 0], hidden_logit))
    at_keys, at_values = (
        pl.ds(pl.multiple_of((first + pl.program_id(1)) * HD, HD), HD) for first in (0, KVH)
    )
    middle = low_ref.shape[1]
    grad_values = jnp.dot(probs.astype(bf16), upstream, preferred_element_type=f32)
    low_ref[0, :, at_values] = grad_values[:middle].astype(bf16)
    high_ref[0, :, at_values] = grad_values[middle:].astype(bf16)
    grad_probs = lax.dot_general(v_ref[0], upstream, last, preferred_element_type=f32)
    mixed = probs * grad_probs
    total = jnp.sum(mixed, axis=0, keepdims=True)
    grad_scores = ((mixed - probs * total) * scale).astype(bf16)
    grad_keys = jnp.dot(grad_scores, query, preferred_element_type=f32)
    low_ref[0, :, at_keys] = grad_keys[:middle].astype(bf16)
    high_ref[0, :, at_keys] = grad_keys[middle:].astype(bf16)
    grad_query = lax.dot_general(
        k_ref[0], grad_scores, (((0,), (0,)), ((), ())), preferred_element_type=f32
    ).T
    for h, at in enumerate(columns):
        gq_ref[0, :, at] = turn_back(
            grad_query[h * count : (h + 1) * count], cos_ref[...], sin_ref[...]
        ).astype(bf16)


def attend_back_call(shift, query, upstream, cosine, sine, kv, kpos, limit, logs):
    rows, count, width = query.shape
    length = kv.shape[1]
    groups = KVH
    many = limit.shape[2]
    part = pl.BlockSpec((1, count, width), lambda r, g, shift: (r, 0, 0))
    fixed = lambda shape: pl.BlockSpec(shape, lambda r, g, shift: (0, 0))
    keys = pl.BlockSpec((1, length, HD), lambda r, g, shift: (r, 0, g))
    values = pl.BlockSpec((1, length, HD), lambda r, g, shift: (r, 0, KVH + g))
    work = rows * groups * length * many
    return pl.pallas_call(
        attend_back_kernel,
        grid_spec=pltpu.PrefetchScalarGridSpec(
            num_scalar_prefetch=1,
            grid=(rows, groups),
            in_specs=[
                part,
                part,
                fixed((count, HD)),
                fixed((count, HD)),
                keys,
                values,
                fixed((length, 1)),
                pl.BlockSpec((1, 1, many), lambda r, g, shift: (r, 0, 0)),
                pl.BlockSpec((1, 1, 1, many), lambda r, g, shift: (r, g, 0, 0)),
            ],
            out_specs=[
                part,
                pl.BlockSpec((1, length // 2, 2 * KVH * HD), lambda r, g, shift: (r, 0, 0)),
                pl.BlockSpec((1, length // 2, 2 * KVH * HD), lambda r, g, shift: (r, 0, 0)),
            ],
        ),
        out_shape=[
            jax.ShapeDtypeStruct((rows, count, width), bf16),
            jax.ShapeDtypeStruct((rows, length // 2, 2 * KVH * HD), bf16),
            jax.ShapeDtypeStruct((rows, length // 2, 2 * KVH * HD), bf16),
        ],
        cost_estimate=pl.CostEstimate(
            flops=10 * work * HD, bytes_accessed=4 * kv.size, transcendentals=work
        ),
        compiler_params=pltpu.CompilerParams(vmem_limit_bytes=vmem_bytes),
        name="attend_back",
    )(shift, query, upstream, cosine, sine, kv, kv, kpos, limit, logs)


def turn_back_kernel(kv_ref, cos_ref, sin_ref, out_ref):
    half = kv_ref.shape[2] // 2
    for at in range(0, half, HD):
        out_ref[0, :, at : at + HD] = turn_back(
            kv_ref[0, :, at : at + HD].astype(f32), cos_ref[...], sin_ref[...]
        ).astype(bf16)
    out_ref[0, :, half:] = kv_ref[0, :, half:]


def turn_back_call(kv, cosine, sine):
    rows, count, width = kv.shape
    row = pl.BlockSpec((1, count, width), lambda r: (r, 0, 0))
    table = pl.BlockSpec((count, HD), lambda r: (0, 0))
    return pl.pallas_call(
        turn_back_kernel,
        grid=(rows,),
        in_specs=[row, table, table],
        out_specs=row,
        out_shape=jax.ShapeDtypeStruct(kv.shape, bf16),
        cost_estimate=pl.CostEstimate(
            flops=4 * kv.size, bytes_accessed=4 * kv.size, transcendentals=0
        ),
        compiler_params=pltpu.CompilerParams(vmem_limit_bytes=vmem_bytes),
        name="turn_back",
    )(kv, cosine, sine)


def matmul(left, right):
    return jnp.dot(left, right, preferred_element_type=f32)


def matmul_nt(left, right):
    return lax.dot_general(left, right, (((1,), (1,)), ((), ())), preferred_element_type=f32)


def matmul_tn(left, right):
    return lax.dot_general(left, right, (((0,), (0,)), ((), ())), preferred_element_type=f32)


def angles(positions):
    inverse_freq = rope_base ** (-jnp.arange(0, HD // 2, dtype=f32) * 2.0 / HD)
    phase = positions[:, None] * inverse_freq[None, :]
    cosine, sine = jnp.cos(phase), jnp.sin(phase)
    return jnp.concatenate([cosine, cosine], -1), jnp.concatenate([-sine, sine], -1)


def norm_back(upstream, normed, inv_rms, gain_row):
    scaled = upstream * gain_row
    return inv_rms * (scaled - normed * jnp.mean(scaled * normed, axis=-1, keepdims=True))


def rms_scale(values):
    return lax.rsqrt(jnp.mean(values * values, axis=-1, keepdims=True) + epsilon)


def local(
    residual,
    out_grad,
    lengths,
    attn_gain,
    query_weight,
    query_bias,
    key_weight,
    key_bias,
    value_weight,
    value_bias,
    output_weight,
    ffn_gain,
    gate_weight,
    up_weight,
    down_weight,
):
    rows, own, width = residual.shape
    tokens = rows * own
    shard = own * lax.axis_size("heads")
    n_heads = lax.axis_size("heads")
    n_seq = lax.axis_size("seq")
    z = lax.axis_index("heads")
    s = lax.axis_index("seq")
    c = lax.axis_index("dp")
    piece = c * n_seq + s
    order_a, order_b = seq_masks()
    depth = gate_weight.shape[0]
    half = n_seq * depth
    q_own = query_weight.shape[1]
    q_all = q_own * n_heads
    kv_width = key_weight.shape[1]
    group_heads = H // KVH

    start = s * shard + z * own
    positions = start + jnp.arange(own, dtype=jnp.int32)
    cosine, sine = angles(positions.astype(f32))

    lanes = Lanes()
    places = seq_places()
    stages = range(len(places).bit_length() - 1)

    def both_cores(mine):
        other = lanes.core(mine)
        full = jnp.zeros((2 * half, mine.shape[1]), bf16)
        full = lax.dynamic_update_slice_in_dim(full, mine, c * half, 0)
        return by_rows(lax.dynamic_update_slice_in_dim(full, other, (1 - c) * half, 0))

    def halves_grad(left, right):
        terms = [
            order.mark(by_rows(matmul_tn(take(left, at, half, 1), order.then(right)).astype(bf16)))
            for at in (1 - c, c)
        ]
        return [terms[1], lanes.core(terms[0])]

    def row_scatter(*arrays):
        items = [
            (lambda p, parts=parts: [take(part, places[p], depth, 0) for part in parts])
            for parts in arrays
        ]
        return SeqScatter(lanes, items, len(places), 0)

    units = gate_weight.shape[1]
    spare = -units % 256
    both = ("dp", "seq")
    down_full, gate_full, up_full = (
        lax.all_gather(jnp.pad(part, ((0, 0), (0, spare))), both, axis=0, tiled=True)
        for part in (down_weight.T, gate_weight, up_weight)
    )

    first_input, kv_own = first_call(
        residual, attn_gain, key_weight, value_weight, key_bias, value_bias, cosine, sine
    )
    kv_ring = lanes.gather(kv_own)
    kv_gather = SeqGather(lanes, jnp.concatenate(kv_ring, axis=1), 1)
    for _ in stages:
        kv_gather.step()
    kv_sent = lanes.sent["seq"][-1]
    kv_all = jnp.concatenate(kv_gather.held, axis=1)
    ring_at = (jnp.arange(n_heads, dtype=jnp.int32) + z) % n_heads
    key_pos = (
        jnp.stack(places)[:, None, None] * shard
        + ring_at[None, :, None] * own
        + jnp.arange(own, dtype=jnp.int32)[None, None, :]
    ).reshape(-1, 1)
    limit = jnp.minimum(positions[None, :], lengths[:, None] - 1)
    limit = jnp.tile(limit, (1, group_heads))[:, None, :]

    extra = 16
    query_half = take(query_weight, c, half, 0)
    bias_rows = jnp.pad(query_bias[None], ((0, extra - 1), (0, 0)))
    query_ring = lanes.gather(jnp.concatenate([query_half, bias_rows], axis=0), kv_ring)
    bias_all = jnp.concatenate([part[half : half + 1] for part in query_ring], axis=1).astype(f32)
    query_rest = both_cores(
        jnp.concatenate([part[:half] for part in after(query_ring[1:], kv_sent)], axis=1)
    )
    output_ring = lanes.gather(take(output_weight, c, half, 1).T, query_ring)
    shift = ((H - z * (q_own // HD)) % H).reshape(1)

    input_flat = first_input.reshape(tokens, width)
    grad_flat = out_grad.reshape(rows, n_heads, own, width).transpose(1, 0, 2, 3)
    grad_flat = grad_flat.reshape(n_heads * tokens, width)
    grad_hidden_all = matmul(grad_flat, down_full)
    input_flat, grad_hidden_all = tie(input_flat, grad_hidden_all)
    query_lin = jnp.concatenate(
        [matmul(input_flat, query_weight), matmul(input_flat, query_rest)], axis=1
    )
    query_lin = (query_lin + bias_all).reshape(rows, own, q_all)
    attended, query_rot, logs = attend_call(
        shift, query_lin, cosine, sine, kv_all, key_pos, limit
    )
    attended = attended.reshape(tokens, q_all)
    output_rest = both_cores(jnp.concatenate(after(output_ring[1:], attended), axis=1))
    stream = residual.astype(f32).reshape(tokens, width)
    second_stream = (
        stream
        + matmul(attended[:, :q_own], output_weight)
        + matmul_nt(attended[:, q_own:], output_rest)
    )
    second_scale = rms_scale(second_stream)
    second_normed = second_stream * second_scale
    second_gain = ffn_gain.astype(f32)
    second_own = (second_normed * second_gain).astype(bf16)

    order = Order()
    order.mark(second_own)
    tokens_ring = [second_own, lanes.ring(second_own)]

    def all_tokens(parts):
        full = jnp.zeros((n_heads * tokens, parts[0].shape[1]), bf16)
        for m, part in enumerate(parts):
            full = lax.dynamic_update_slice_in_dim(full, part, (z + m) % n_heads * tokens, 0)
        return by_rows(full)

    hidden_parts, gate_parts, up_parts, back_parts = [], [], [], []
    for m in range(n_heads):
        part = order.then(tokens_ring[m])
        if m > 0:
            part, back_parts[m - 1] = tie(part, back_parts[m - 1])
            tokens_ring[m] = part
        if 0 < m < n_heads - 1:
            tokens_ring.append(lanes.ring(part))
        grad_hidden = take(grad_hidden_all, (z + m) % n_heads, tokens, 0)
        gate_act = matmul(part, gate_full)
        up_act = matmul(part, up_full)
        sigmoid_gate = jax.nn.sigmoid(gate_act)
        silu_gate = gate_act * sigmoid_gate
        hidden_parts.append(by_rows((silu_gate * up_act).astype(bf16)))
        gate_parts.append(
            by_rows(
                (
                    grad_hidden * up_act * sigmoid_gate * (1.0 + gate_act * (1.0 - sigmoid_gate))
                ).astype(bf16)
            )
        )
        up_parts.append(by_rows((grad_hidden * silu_gate).astype(bf16)))
        back = matmul_nt(gate_parts[m], gate_full) + matmul_nt(up_parts[m], up_full)
        back_parts.append(order.mark(back.astype(bf16)))
    back_all = order.mark(all_tokens(back_parts))
    second_back = lax.psum_scatter(back_all, "heads", scatter_dimension=0, tiled=True)

    hidden = order.mark(all_tokens(order.then(hidden_parts)))
    down_terms = halves_grad(grad_flat, hidden)
    ffn_part = order.mark(matmul_nt(order.then(hidden), down_full).astype(bf16))
    ffn_own = lax.psum_scatter(
        after(ffn_part, back_all), "heads", scatter_dimension=0, tiled=True
    )
    block_out = (second_stream + ffn_own.astype(f32)).reshape(rows, own, width)
    second_input = order.mark(all_tokens(order.then(tokens_ring)))
    gate_terms = halves_grad(second_input, all_tokens(order.then(gate_parts)))
    down_scatter = row_scatter(order.then(down_terms)).step()
    order.mark(lanes.sent["seq"][-1])
    up_terms = halves_grad(second_input, all_tokens(order.then(up_parts)))
    (down_sum,) = down_scatter.terms()
    down_grad = total_of(down_sum)[:, :units]
    both_scatter = row_scatter(order.then(gate_terms), order.then(up_terms)).step()

    second_back = order.then(second_back).astype(f32)
    second_gain_term = jnp.sum(second_back * second_normed, axis=0)
    grad_own = take(out_grad, z, own, 1).reshape(tokens, width).astype(f32)
    grad_stream = grad_own + norm_back(second_back, second_normed, second_scale, second_gain)
    grad_attn = grad_stream.astype(bf16)

    grad_attended = jnp.concatenate(
        [matmul_nt(grad_attn, output_weight), matmul(grad_attn, output_rest)], axis=1
    ).astype(bf16)
    grad_query, kv_low, kv_high = attend_back_call(
        shift,
        query_rot,
        grad_attended.reshape(rows, own, q_all),
        cosine,
        sine,
        kv_all,
        key_pos,
        limit,
        logs,
    )
    order.mark(grad_query)
    grad_query = grad_query.reshape(tokens, q_all)
    kv_scatter = SeqScatter(
        lanes,
        [lambda p: [take((kv_low, kv_high)[p // (n_seq // 2)], p % (n_seq // 2), shard, 1)]],
        n_seq,
        1,
    ).step(kv_high)
    query_terms = halves_grad(input_flat, grad_query)
    output_terms = halves_grad(grad_attn, attended)
    (kv_terms,) = kv_scatter.terms()

    kv_sum = total_of(order.then(kv_terms)).astype(bf16)
    kv_away = order.mark(
        [take(kv_sum, m, own, 1) for m in range(1, n_heads)]
    )
    kv_came = lanes.direct(kv_away, True)

    qo_scatter = row_scatter(order.then(query_terms), order.then(output_terms)).step()
    first_scale = rms_scale(stream)
    first_normed = stream * first_scale
    first_gain = attn_gain.astype(f32)
    first_back = order.mark(
        matmul_nt(order.then(grad_query[:, :q_own]), query_weight)
        + matmul_nt(order.then(grad_query[:, q_own:]), query_rest)
    )
    grad_kv = turn_back_call(
        total_of([take(kv_sum, 0, own, 1)] + order.then(kv_came)).astype(bf16), cosine, sine
    )
    grad_kv = order.mark(grad_kv.reshape(tokens, 2 * kv_width))

    first_back = (
        first_back
        + matmul_nt(grad_kv[:, :kv_width], key_weight)
        + matmul_nt(grad_kv[:, kv_width:], value_weight)
    )
    first_gain_term = jnp.sum(first_back * first_normed, axis=0)

    small = jnp.concatenate(
        [
            first_gain_term,
            second_gain_term,
            jnp.roll(jnp.sum(grad_query.astype(f32), axis=0), z * q_own),
            jnp.sum(grad_kv.astype(f32), axis=0),
        ]
    )
    kv_cut = kv_width // n_heads
    packed = 2 * kv_width
    lines = -(-small.size // (packed * 16)) * 16
    small = as_sent(jnp.pad(small, (0, lines * packed - small.size)).reshape(lines, packed))

    def with_small(value):
        return jnp.concatenate([value, small.astype(bf16)], axis=0)

    def apart(value):
        return value[:-lines], value[-lines:].astype(f32)

    kv_mine, kv_other = (
        matmul_tn(take(input_flat, at, half, 1), grad_kv).astype(bf16) for at in (c, 1 - c)
    )
    kv_other, came_small = apart(lanes.core(with_small(kv_other)))
    small = as_sent(small + came_small)
    kv_terms = [[take(part, place, depth, 0) for part in (kv_mine, kv_other)] for place in places]
    while len(kv_terms) > 1:
        count = len(kv_terms) // 2
        message = join([low_total(terms) for terms in kv_terms[count:]], 0)
        came, came_small = apart(lanes.seq(with_small(message), count.bit_length() - 1))
        small = as_sent(small + came_small)
        kv_terms = [terms + [came[p * depth : (p + 1) * depth]] for p, terms in enumerate(kv_terms[:count])]
    kv_part = low_total(kv_terms[0])
    low_small = small.astype(bf16).reshape(-1, 2 * kv_cut)
    kv_pieces = [
        jnp.concatenate(
            [
                take(part, (z + m) % n_heads, kv_cut, 1)
                for part in (kv_part[:, :kv_width], kv_part[:, kv_width:])
            ],
            axis=1,
        )
        for m in range(n_heads)
    ]
    came = lanes.direct(
        [jnp.concatenate([part, low_small], axis=0) for part in kv_pieces[1:]], True
    )
    kv_total = total_of([kv_pieces[0]] + [part[:depth] for part in came])
    sums = total_of([low_small] + [part[depth:] for part in came])
    sums = sums.reshape(-1)
    residual_grad = grad_stream + norm_back(first_back, first_normed, first_scale, first_gain)

    query_sum, output_sum = (low_total(terms) for terms in qo_scatter.terms())
    gate_grad, up_grad = (total_of(terms)[:, :units] for terms in both_scatter.terms())
    qo_parts = [
        jnp.concatenate(pair, axis=1)
        for pair in zip(split(query_sum, n_heads, 1), split(output_sum, n_heads, 1))
    ]
    qo_grad = total_of(qo_parts[:1] + lanes.direct(qo_parts[1:], True))
    query_weight_grad = qo_grad[:, :q_own]
    output_weight_grad = qo_grad[:, q_own:].T

    gain_piece = width // (lax.axis_size("dp") * n_seq * n_heads)
    gain_at = (piece * n_heads + z) * gain_piece
    attn_gain_grad = lax.dynamic_slice_in_dim(sums, gain_at, gain_piece, 0)
    ffn_gain_grad = lax.dynamic_slice_in_dim(sums, width + gain_at, gain_piece, 0)
    query_bias_grad = lax.dynamic_slice_in_dim(sums, 2 * width + z * q_own, q_own, 0)
    kv_at = 2 * width + q_all + z * kv_cut
    key_bias_grad = lax.dynamic_slice_in_dim(sums, kv_at, kv_cut, 0)
    value_bias_grad = lax.dynamic_slice_in_dim(sums, kv_at + kv_width, kv_cut, 0)

    return (
        block_out.astype(bf16),
        residual_grad.reshape(rows, own, width),
        attn_gain_grad,
        query_weight_grad,
        query_bias_grad,
        kv_total[:, :kv_cut],
        key_bias_grad,
        kv_total[:, kv_cut:],
        value_bias_grad,
        output_weight_grad,
        ffn_gain_grad,
        gate_grad,
        up_grad,
        down_grad.T,
    )


def solution(mesh):
    in_specs = (
        P("dp", ("seq", "heads"), None),
        P("dp", "seq", None),
        P("dp"),
        P(),
        P(None, "heads"),
        P("heads"),
        P(),
        P(),
        P(),
        P(),
        P("heads", None),
        P(),
        P(("dp", "seq"), "heads"),
        P(("dp", "seq"), "heads"),
        P("heads", ("dp", "seq")),
    )
    out_specs = (
        P("dp", ("seq", "heads"), None),
        P("dp", ("seq", "heads"), None),
        P(("dp", "seq", "heads")),
        P(("dp", "seq"), "heads"),
        P("heads"),
        P(("dp", "seq"), "heads"),
        P("heads"),
        P(("dp", "seq"), "heads"),
        P("heads"),
        P("heads", ("dp", "seq")),
        P(("dp", "seq", "heads")),
        P(("dp", "seq"), "heads"),
        P(("dp", "seq"), "heads"),
        P("heads", ("dp", "seq")),
    )
    return jax.shard_map(local, mesh=mesh, in_specs=in_specs, out_specs=out_specs, check_vma=False)
```

```python
import jax
import jax.numpy as jnp
from jax import lax
from jax.experimental import pallas as pl
from jax.experimental.layout import Layout, with_layout_constraint
from jax.experimental.pallas import tpu as pltpu
from jax.sharding import PartitionSpec as P

H = 12
KVH = 2
HD = 128

epsilon = 1e-06
rope_base = 1000000.0
hidden_logit = -1e30
log2_e = 1.4426950408889634

bf16 = jnp.bfloat16
f32 = jnp.float32
vmem_bytes = 48 * 2**20


def after(value, earlier):
    return lax.optimization_barrier((value, earlier))[0]


def tie(*values):
    return lax.optimization_barrier(values)


def swap(value, axis, mask):
    pairs = [(source, source ^ mask) for source in range(lax.axis_size(axis))]
    return lax.ppermute(value, axis, pairs)


def rotate_down(value, axis):
    size = lax.axis_size(axis)
    pairs = [(source, (source - 1) % size) for source in range(size)]
    return lax.ppermute(value, axis, pairs)


class Lanes:
    def __init__(self):
        self.sent = {}
        self.came = {}

    def send(self, key, value, move):
        sent, came = self.sent.setdefault(key, []), self.came.setdefault(key, [])
        if sent:
            value = after(value, (sent[-1], came[-2:][0]) if len(came) > 1 else sent[-1])
        sent.append(value)
        came.append(move(value))
        return came[-1]

    def seq(self, value, stage):
        size = lax.axis_size("seq")
        pairs = [
            (core * size + place, core * size + (place ^ masks[stage]))
            for core, masks in enumerate(seq_masks())
            for place in range(size)
        ]
        return self.send("seq", value, lambda v: lax.ppermute(v, ("dp", "seq"), pairs))

    def core(self, value):
        return self.send("dp", value, lambda v: swap(v, "dp", 1))

    def direct(self, values, away, gate=None):
        size = lax.axis_size("heads")
        if gate is not None:
            values = after(values, gate)
        return [
            lax.ppermute(
                value, "heads", [(i, (i + m if away else i - m) % size) for i in range(size)]
            )
            for m, value in enumerate(values, 1)
        ]

    def gather(self, block, gate=None):
        return [block] + self.direct([block] * (lax.axis_size("heads") - 1), False, gate)

    def ring(self, value):
        return self.send("heads", value, lambda v: rotate_down(v, "heads"))


class Order:
    def __init__(self):
        self.last = None

    def then(self, value):
        return value if self.last is None else after(value, self.last)

    def mark(self, value):
        self.last = value
        return value


def total_of(parts):
    result = parts[0].astype(f32)
    for part in parts[1:]:
        result = result + part.astype(f32)
    return result


def low_total(parts):
    return parts[0] if len(parts) == 1 else total_of(parts).astype(bf16)


def as_sent(sums):
    return lax.reduce_precision(sums, exponent_bits=8, mantissa_bits=7)


def join(parts, dim):
    return parts[0] if len(parts) == 1 else jnp.concatenate(parts, axis=dim)


def split(value, count, dim):
    return [value] if count == 1 else jnp.split(value, count, axis=dim)


def seq_masks():
    bits = lax.axis_size("seq").bit_length() - 1
    masks = [1 << bit for bit in range(bits)]
    return masks, masks[bits // 2 :] + masks[: bits // 2]


def seq_places():
    at = []
    for masks in seq_masks():
        mixed = [0]
        for mask in masks:
            mixed += [m ^ mask for m in mixed]
        at.append(mixed)
    s, c = lax.axis_index("seq"), lax.axis_index("dp")
    return [s ^ jnp.where(c == 0, first, second) for first, second in zip(*at)]


class SeqGather:
    def __init__(self, lanes, block, dim):
        self.lanes, self.held, self.dim, self.stage = lanes, [block], dim, 0

    def step(self):
        came = self.lanes.seq(join(self.held, self.dim), self.stage)
        self.held = self.held + [came]
        self.stage += 1
        return self

    def blocks(self, gate):
        parts, count = [], 1
        for index, part in enumerate(after(self.held, gate)):
            parts += split(part, count, self.dim)
            count *= 2 if index else 1
        return parts


class SeqScatter:
    def __init__(self, lanes, items, count, dim):
        self.lanes, self.items, self.count, self.dim = lanes, items, count, dim
        self.came = []

    def at(self, i, p):
        return self.items[i](p) + [came[i][p] for came in self.came]

    def step(self, message=None):
        half = self.count // 2
        each = range(len(self.items))
        if message is None:
            message = join(
                [low_total(self.at(i, p)) for i in each for p in range(half, self.count)],
                self.dim,
            )
        came = self.lanes.seq(message, half.bit_length() - 1)
        parts = split(came, half * len(self.items), self.dim)
        self.came.append([parts[i * half : (i + 1) * half] for i in each])
        self.count = half
        return self

    def terms(self):
        while self.count > 1:
            self.step()
        return [self.at(i, 0) for i in range(len(self.items))]


def by_rows(value):
    return with_layout_constraint(value, Layout(major_to_minor=tuple(range(value.ndim))))


def take(value, index, size, dim):
    return lax.dynamic_slice_in_dim(value, index * size, size, dim)


def turn(values, cosine, sine):
    return values * cosine + pltpu.roll(values, HD // 2, 1) * sine


def turn_back(values, cosine, sine):
    return values * cosine - pltpu.roll(values, HD // 2, 1) * sine


def first_kernel(x_ref, gain_ref, kw_ref, vw_ref, kb_ref, vb_ref, cos_ref, sin_ref, in_ref, kv_ref):
    x = x_ref[0].astype(f32)
    scale = lax.rsqrt(jnp.mean(x * x, axis=-1, keepdims=True) + epsilon)
    low = (x * scale * gain_ref[...].astype(f32)).astype(bf16)
    in_ref[0] = low
    width = kw_ref.shape[1]
    keys = jnp.dot(low, kw_ref[...], preferred_element_type=f32) + kb_ref[...].astype(f32)
    for at in range(0, width, HD):
        kv_ref[0, :, at : at + HD] = turn(
            keys[:, at : at + HD], cos_ref[...], sin_ref[...]
        ).astype(bf16)
    values = jnp.dot(low, vw_ref[...], preferred_element_type=f32) + vb_ref[...].astype(f32)
    kv_ref[0, :, width:] = values.astype(bf16)


def first_call(residual, gain, kw, vw, kb, vb, cosine, sine):
    rows, count, width = residual.shape
    kv = kw.shape[1]
    fixed = lambda shape: pl.BlockSpec(shape, lambda r: (0, 0))
    row = lambda size: pl.BlockSpec((1, count, size), lambda r: (r, 0, 0))
    return pl.pallas_call(
        first_kernel,
        grid=(rows,),
        in_specs=[
            row(width),
            fixed((1, width)),
            fixed((width, kv)),
            fixed((width, kv)),
            fixed((1, kv)),
            fixed((1, kv)),
            fixed((count, HD)),
            fixed((count, HD)),
        ],
        out_specs=[row(width), row(2 * kv)],
        out_shape=[
            jax.ShapeDtypeStruct((rows, count, width), bf16),
            jax.ShapeDtypeStruct((rows, count, 2 * kv), bf16),
        ],
        cost_estimate=pl.CostEstimate(
            flops=4 * rows * count * width * kv,
            bytes_accessed=2 * (2 * rows * count * width + 2 * width * kv),
            transcendentals=0,
        ),
        compiler_params=pltpu.CompilerParams(vmem_limit_bytes=vmem_bytes),
        name="first_norm",
    )(residual, gain[None], kw, vw, kb[None], vb[None], cosine, sine)


def head_columns(shift_ref, width):
    heads = width // HD
    first = pl.program_id(1) * (heads // KVH) + shift_ref[0]
    places = [lax.rem(first + h, heads) for h in range(heads // KVH)]
    return [pl.ds(pl.multiple_of(place * HD, HD), HD) for place in places]


def attend_kernel(
    shift_ref,
    q_ref,
    cos_ref,
    sin_ref,
    k_ref,
    v_ref,
    kpos_ref,
    limit_ref,
    out_ref,
    turned_ref,
    log_ref,
):
    count = q_ref.shape[1]
    columns = head_columns(shift_ref, q_ref.shape[2])
    turned = []
    for at in columns:
        u = turn(q_ref[0, :, at], cos_ref[...], sin_ref[...])
        turned_ref[0, :, at] = u.astype(bf16)
        turned.append(u)
    query = jnp.concatenate(turned, axis=0).astype(bf16)
    scores = lax.dot_general(
        k_ref[0], query, (((1,), (1,)), ((), ())), preferred_element_type=f32
    )
    seen = kpos_ref[...] <= limit_ref[0]
    scores = jnp.where(seen, scores * (HD**-0.5 * log2_e), hidden_logit)
    peak = jnp.max(scores, axis=0, keepdims=True)
    weight = jnp.exp2(scores - peak)
    total = jnp.sum(weight, axis=0, keepdims=True)
    log_ref[0, 0] = peak + jnp.log2(total)
    out = lax.dot_general(
        v_ref[0], weight.astype(bf16), (((0,), (0,)), ((), ())), preferred_element_type=f32
    )
    out = (out * (1.0 / total)).T
    for h, at in enumerate(columns):
        out_ref[0, :, at] = out[h * count : (h + 1) * count].astype(bf16)


def attend_call(shift, query, cosine, sine, kv, kpos, limit):
    rows, count, width = query.shape
    length = kv.shape[1]
    groups = KVH
    many = limit.shape[2]
    part = pl.BlockSpec((1, count, width), lambda r, g, shift: (r, 0, 0))
    fixed = lambda shape: pl.BlockSpec(shape, lambda r, g, shift: (0, 0))
    keys = pl.BlockSpec((1, length, HD), lambda r, g, shift: (r, 0, g))
    values = pl.BlockSpec((1, length, HD), lambda r, g, shift: (r, 0, KVH + g))
    work = rows * groups * length * many
    return pl.pallas_call(
        attend_kernel,
        grid_spec=pltpu.PrefetchScalarGridSpec(
            num_scalar_prefetch=1,
            grid=(rows, groups),
            in_specs=[
                part,
                fixed((count, HD)),
                fixed((count, HD)),
                keys,
                values,
                fixed((length, 1)),
                pl.BlockSpec((1, 1, many), lambda r, g, shift: (r, 0, 0)),
            ],
            out_specs=[part, part, pl.BlockSpec((1, 1, 1, many), lambda r, g, shift: (r, g, 0, 0))],
        ),
        out_shape=[
            jax.ShapeDtypeStruct((rows, count, width), bf16),
            jax.ShapeDtypeStruct((rows, count, width), bf16),
            jax.ShapeDtypeStruct((rows, groups, 1, many), f32),
        ],
        cost_estimate=pl.CostEstimate(
            flops=4 * work * HD, bytes_accessed=2 * kv.size, transcendentals=work
        ),
        compiler_params=pltpu.CompilerParams(vmem_limit_bytes=vmem_bytes),
        name="attend",
    )(shift, query, cosine, sine, kv, kv, kpos, limit)


def attend_back_kernel(
    shift_ref,
    q_ref,
    og_ref,
    cos_ref,
    sin_ref,
    k_ref,
    v_ref,
    kpos_ref,
    limit_ref,
    log_ref,
    gq_ref,
    low_ref,
    high_ref,
):
    count = q_ref.shape[1]
    columns = head_columns(shift_ref, q_ref.shape[2])

    def rows_of(ref):
        parts = [ref[0, :, at].astype(f32) for at in columns]
        return jnp.concatenate(parts, axis=0).astype(bf16)

    query, upstream = rows_of(q_ref), rows_of(og_ref)
    last = (((1,), (1,)), ((), ()))
    scores = lax.dot_general(k_ref[0], query, last, preferred_element_type=f32)
    seen = kpos_ref[...] <= limit_ref[0]
    scale = HD**-0.5
    probs = jnp.exp2(jnp.where(seen, scores * (scale * log2_e) - log_ref[0, 0], hidden_logit))
    at_keys, at_values = (
        pl.ds(pl.multiple_of((first + pl.program_id(1)) * HD, HD), HD) for first in (0, KVH)
    )
    middle = low_ref.shape[1]
    grad_values = jnp.dot(probs.astype(bf16), upstream, preferred_element_type=f32)
    low_ref[0, :, at_values] = grad_values[:middle].astype(bf16)
    high_ref[0, :, at_values] = grad_values[middle:].astype(bf16)
    grad_probs = lax.dot_general(v_ref[0], upstream, last, preferred_element_type=f32)
    mixed = probs * grad_probs
    total = jnp.sum(mixed, axis=0, keepdims=True)
    grad_scores = ((mixed - probs * total) * scale).astype(bf16)
    grad_keys = jnp.dot(grad_scores, query, preferred_element_type=f32)
    low_ref[0, :, at_keys] = grad_keys[:middle].astype(bf16)
    high_ref[0, :, at_keys] = grad_keys[middle:].astype(bf16)
    grad_query = lax.dot_general(
        k_ref[0], grad_scores, (((0,), (0,)), ((), ())), preferred_element_type=f32
    ).T
    for h, at in enumerate(columns):
        gq_ref[0, :, at] = turn_back(
            grad_query[h * count : (h + 1) * count], cos_ref[...], sin_ref[...]
        ).astype(bf16)


def attend_back_call(shift, query, upstream, cosine, sine, kv, kpos, limit, logs):
    rows, count, width = query.shape
    length = kv.shape[1]
    groups = KVH
    many = limit.shape[2]
    part = pl.BlockSpec((1, count, width), lambda r, g, shift: (r, 0, 0))
    fixed = lambda shape: pl.BlockSpec(shape, lambda r, g, shift: (0, 0))
    keys = pl.BlockSpec((1, length, HD), lambda r, g, shift: (r, 0, g))
    values = pl.BlockSpec((1, length, HD), lambda r, g, shift: (r, 0, KVH + g))
    work = rows * groups * length * many
    return pl.pallas_call(
        attend_back_kernel,
        grid_spec=pltpu.PrefetchScalarGridSpec(
            num_scalar_prefetch=1,
            grid=(rows, groups),
            in_specs=[
                part,
                part,
                fixed((count, HD)),
                fixed((count, HD)),
                keys,
                values,
                fixed((length, 1)),
                pl.BlockSpec((1, 1, many), lambda r, g, shift: (r, 0, 0)),
                pl.BlockSpec((1, 1, 1, many), lambda r, g, shift: (r, g, 0, 0)),
            ],
            out_specs=[
                part,
                pl.BlockSpec((1, length // 2, 2 * KVH * HD), lambda r, g, shift: (r, 0, 0)),
                pl.BlockSpec((1, length // 2, 2 * KVH * HD), lambda r, g, shift: (r, 0, 0)),
            ],
        ),
        out_shape=[
            jax.ShapeDtypeStruct((rows, count, width), bf16),
            jax.ShapeDtypeStruct((rows, length // 2, 2 * KVH * HD), bf16),
            jax.ShapeDtypeStruct((rows, length // 2, 2 * KVH * HD), bf16),
        ],
        cost_estimate=pl.CostEstimate(
            flops=10 * work * HD, bytes_accessed=4 * kv.size, transcendentals=work
        ),
        compiler_params=pltpu.CompilerParams(vmem_limit_bytes=vmem_bytes),
        name="attend_back",
    )(shift, query, upstream, cosine, sine, kv, kv, kpos, limit, logs)


def turn_back_kernel(kv_ref, cos_ref, sin_ref, out_ref):
    half = kv_ref.shape[2] // 2
    for at in range(0, half, HD):
        out_ref[0, :, at : at + HD] = turn_back(
            kv_ref[0, :, at : at + HD].astype(f32), cos_ref[...], sin_ref[...]
        ).astype(bf16)
    out_ref[0, :, half:] = kv_ref[0, :, half:]


def turn_back_call(kv, cosine, sine):
    rows, count, width = kv.shape
    row = pl.BlockSpec((1, count, width), lambda r: (r, 0, 0))
    table = pl.BlockSpec((count, HD), lambda r: (0, 0))
    return pl.pallas_call(
        turn_back_kernel,
        grid=(rows,),
        in_specs=[row, table, table],
        out_specs=row,
        out_shape=jax.ShapeDtypeStruct(kv.shape, bf16),
        cost_estimate=pl.CostEstimate(
            flops=4 * kv.size, bytes_accessed=4 * kv.size, transcendentals=0
        ),
        compiler_params=pltpu.CompilerParams(vmem_limit_bytes=vmem_bytes),
        name="turn_back",
    )(kv, cosine, sine)


def matmul(left, right):
    return jnp.dot(left, right, preferred_element_type=f32)


def matmul_nt(left, right):
    return lax.dot_general(left, right, (((1,), (1,)), ((), ())), preferred_element_type=f32)


def matmul_tn(left, right):
    return lax.dot_general(left, right, (((0,), (0,)), ((), ())), preferred_element_type=f32)


def angles(positions):
    inverse_freq = rope_base ** (-jnp.arange(0, HD // 2, dtype=f32) * 2.0 / HD)
    phase = positions[:, None] * inverse_freq[None, :]
    cosine, sine = jnp.cos(phase), jnp.sin(phase)
    return jnp.concatenate([cosine, cosine], -1), jnp.concatenate([-sine, sine], -1)


def norm_back(upstream, normed, inv_rms, gain_row):
    scaled = upstream * gain_row
    return inv_rms * (scaled - normed * jnp.mean(scaled * normed, axis=-1, keepdims=True))


def rms_scale(values):
    return lax.rsqrt(jnp.mean(values * values, axis=-1, keepdims=True) + epsilon)


def local(
    residual,
    out_grad,
    lengths,
    attn_gain,
    query_weight,
    query_bias,
    key_weight,
    key_bias,
    value_weight,
    value_bias,
    output_weight,
    ffn_gain,
    gate_weight,
    up_weight,
    down_weight,
):
    rows, own, width = residual.shape
    tokens = rows * own
    shard = own * lax.axis_size("heads")
    n_heads = lax.axis_size("heads")
    n_seq = lax.axis_size("seq")
    z = lax.axis_index("heads")
    s = lax.axis_index("seq")
    c = lax.axis_index("dp")
    piece = c * n_seq + s
    order_a, order_b = seq_masks()
    depth = gate_weight.shape[0]
    half = n_seq * depth
    q_own = query_weight.shape[1]
    q_all = q_own * n_heads
    kv_width = key_weight.shape[1]
    group_heads = H // KVH

    start = s * shard + z * own
    positions = start + jnp.arange(own, dtype=jnp.int32)
    cosine, sine = angles(positions.astype(f32))

    lanes = Lanes()
    places = seq_places()
    stages = range(len(places).bit_length() - 1)

    def both_cores(mine):
        other = lanes.core(mine)
        full = jnp.zeros((2 * half, mine.shape[1]), bf16)
        full = lax.dynamic_update_slice_in_dim(full, mine, c * half, 0)
        return by_rows(lax.dynamic_update_slice_in_dim(full, other, (1 - c) * half, 0))

    def halves_grad(left, right):
        terms = [
            order.mark(by_rows(matmul_tn(take(left, at, half, 1), order.then(right)).astype(bf16)))
            for at in (1 - c, c)
        ]
        return [terms[1], lanes.core(terms[0])]

    def row_scatter(*arrays):
        items = [
            (lambda p, parts=parts: [take(part, places[p], depth, 0) for part in parts])
            for parts in arrays
        ]
        return SeqScatter(lanes, items, len(places), 0)

    units = gate_weight.shape[1]
    spare = -units % 256
    both = ("dp", "seq")
    down_full, gate_full, up_full = (
        lax.all_gather(jnp.pad(part, ((0, 0), (0, spare))), both, axis=0, tiled=True)
        for part in (down_weight.T, gate_weight, up_weight)
    )

    first_input, kv_own = first_call(
        residual, attn_gain, key_weight, value_weight, key_bias, value_bias, cosine, sine
    )
    kv_ring = lanes.gather(kv_own)
    kv_gather = SeqGather(lanes, jnp.concatenate(kv_ring, axis=1), 1)
    for _ in stages:
        kv_gather.step()
    kv_sent = lanes.sent["seq"][-1]
    kv_all = jnp.concatenate(kv_gather.held, axis=1)
    ring_at = (jnp.arange(n_heads, dtype=jnp.int32) + z) % n_heads
    key_pos = (
        jnp.stack(places)[:, None, None] * shard
        + ring_at[None, :, None] * own
        + jnp.arange(own, dtype=jnp.int32)[None, None, :]
    ).reshape(-1, 1)
    limit = jnp.minimum(positions[None, :], lengths[:, None] - 1)
    limit = jnp.tile(limit, (1, group_heads))[:, None, :]

    extra = 16
    query_half = take(query_weight, c, half, 0)
    bias_rows = jnp.pad(query_bias[None], ((0, extra - 1), (0, 0)))
    query_ring = lanes.gather(jnp.concatenate([query_half, bias_rows], axis=0), kv_ring)
    bias_all = jnp.concatenate([part[half : half + 1] for part in query_ring], axis=1).astype(f32)
    query_rest = both_cores(
        jnp.concatenate([part[:half] for part in after(query_ring[1:], kv_sent)], axis=1)
    )
    output_ring = lanes.gather(take(output_weight, c, half, 1).T, query_ring)
    shift = ((H - z * (q_own // HD)) % H).reshape(1)

    input_flat = first_input.reshape(tokens, width)
    grad_flat = out_grad.reshape(rows, n_heads, own, width).transpose(1, 0, 2, 3)
    grad_flat = grad_flat.reshape(n_heads * tokens, width)
    grad_hidden_all = matmul(grad_flat, down_full)
    input_flat, grad_hidden_all = tie(input_flat, grad_hidden_all)
    query_lin = jnp.concatenate(
        [matmul(input_flat, query_weight), matmul(input_flat, query_rest)], axis=1
    )
    query_lin = (query_lin + bias_all).reshape(rows, own, q_all)
    attended, query_rot, logs = attend_call(
        shift, query_lin, cosine, sine, kv_all, key_pos, limit
    )
    attended = attended.reshape(tokens, q_all)
    output_rest = both_cores(jnp.concatenate(after(output_ring[1:], attended), axis=1))
    stream = residual.astype(f32).reshape(tokens, width)
    second_stream = (
        stream
        + matmul(attended[:, :q_own], output_weight)
        + matmul_nt(attended[:, q_own:], output_rest)
    )
    second_scale = rms_scale(second_stream)
    second_normed = second_stream * second_scale
    second_gain = ffn_gain.astype(f32)
    second_own = (second_normed * second_gain).astype(bf16)

    order = Order()
    order.mark(second_own)
    tokens_ring = [second_own, lanes.ring(second_own)]

    def all_tokens(parts):
        full = jnp.zeros((n_heads * tokens, parts[0].shape[1]), bf16)
        for m, part in enumerate(parts):
            full = lax.dynamic_update_slice_in_dim(full, part, (z + m) % n_heads * tokens, 0)
        return by_rows(full)

    hidden_parts, gate_parts, up_parts, back_parts = [], [], [], []
    for m in range(n_heads):
        part = order.then(tokens_ring[m])
        if m > 0:
            part, back_parts[m - 1] = tie(part, back_parts[m - 1])
            tokens_ring[m] = part
        if 0 < m < n_heads - 1:
            tokens_ring.append(lanes.ring(part))
        grad_hidden = take(grad_hidden_all, (z + m) % n_heads, tokens, 0)
        gate_act = matmul(part, gate_full)
        up_act = matmul(part, up_full)
        sigmoid_gate = jax.nn.sigmoid(gate_act)
        silu_gate = gate_act * sigmoid_gate
        hidden_parts.append(by_rows((silu_gate * up_act).astype(bf16)))
        gate_parts.append(
            by_rows(
                (
                    grad_hidden * up_act * sigmoid_gate * (1.0 + gate_act * (1.0 - sigmoid_gate))
                ).astype(bf16)
            )
        )
        up_parts.append(by_rows((grad_hidden * silu_gate).astype(bf16)))
        back = matmul_nt(gate_parts[m], gate_full) + matmul_nt(up_parts[m], up_full)
        back_parts.append(order.mark(back.astype(bf16)))
    back_all = order.mark(all_tokens(back_parts))
    second_back = lax.psum_scatter(back_all, "heads", scatter_dimension=0, tiled=True)

    hidden = order.mark(all_tokens(order.then(hidden_parts)))
    down_terms = halves_grad(grad_flat, hidden)
    ffn_part = order.mark(matmul_nt(order.then(hidden), down_full).astype(bf16))
    ffn_own = lax.psum_scatter(
        after(ffn_part, back_all), "heads", scatter_dimension=0, tiled=True
    )
    block_out = (second_stream + ffn_own.astype(f32)).reshape(rows, own, width)
    second_input = order.mark(all_tokens(order.then(tokens_ring)))
    gate_terms = halves_grad(second_input, all_tokens(order.then(gate_parts)))
    down_scatter = row_scatter(order.then(down_terms)).step()
    order.mark(lanes.sent["seq"][-1])
    up_terms = halves_grad(second_input, all_tokens(order.then(up_parts)))
    (down_sum,) = down_scatter.terms()
    down_grad = total_of(down_sum)[:, :units]
    both_scatter = row_scatter(order.then(gate_terms), order.then(up_terms)).step()

    second_back = order.then(second_back).astype(f32)
    second_gain_term = jnp.sum(second_back * second_normed, axis=0)
    grad_own = take(out_grad, z, own, 1).reshape(tokens, width).astype(f32)
    grad_stream = grad_own + norm_back(second_back, second_normed, second_scale, second_gain)
    grad_attn = grad_stream.astype(bf16)

    grad_attended = jnp.concatenate(
        [matmul_nt(grad_attn, output_weight), matmul(grad_attn, output_rest)], axis=1
    ).astype(bf16)
    grad_query, kv_low, kv_high = attend_back_call(
        shift,
        query_rot,
        grad_attended.reshape(rows, own, q_all),
        cosine,
        sine,
        kv_all,
        key_pos,
        limit,
        logs,
    )
    order.mark(grad_query)
    grad_query = grad_query.reshape(tokens, q_all)
    kv_scatter = SeqScatter(
        lanes,
        [lambda p: [take((kv_low, kv_high)[p // (n_seq // 2)], p % (n_seq // 2), shard, 1)]],
        n_seq,
        1,
    ).step(kv_high)
    kv_scatter.came[0], both_scatter.came[0] = tie(kv_scatter.came[0], both_scatter.came[0])
    query_terms = halves_grad(input_flat, grad_query)
    output_terms = halves_grad(grad_attn, attended)
    (kv_terms,) = kv_scatter.terms()

    kv_sum = total_of(order.then(kv_terms)).astype(bf16)
    kv_away = order.mark(
        [take(kv_sum, m, own, 1) for m in range(1, n_heads)]
    )
    kv_came = lanes.direct(kv_away, True)

    qo_scatter = row_scatter(order.then(query_terms), order.then(output_terms)).step()
    first_scale = rms_scale(stream)
    first_normed = stream * first_scale
    first_gain = attn_gain.astype(f32)
    first_back = order.mark(
        matmul_nt(order.then(grad_query[:, :q_own]), query_weight)
        + matmul_nt(order.then(grad_query[:, q_own:]), query_rest)
    )
    grad_kv = turn_back_call(
        total_of([take(kv_sum, 0, own, 1)] + order.then(kv_came)).astype(bf16), cosine, sine
    )
    grad_kv = order.mark(grad_kv.reshape(tokens, 2 * kv_width))

    first_back = (
        first_back
        + matmul_nt(grad_kv[:, :kv_width], key_weight)
        + matmul_nt(grad_kv[:, kv_width:], value_weight)
    )
    first_gain_term = jnp.sum(first_back * first_normed, axis=0)

    small = jnp.concatenate(
        [
            first_gain_term,
            second_gain_term,
            jnp.roll(jnp.sum(grad_query.astype(f32), axis=0), z * q_own),
            jnp.sum(grad_kv.astype(f32), axis=0),
        ]
    )
    kv_cut = kv_width // n_heads
    packed = 2 * kv_width
    lines = -(-small.size // (packed * 16)) * 16
    small = as_sent(jnp.pad(small, (0, lines * packed - small.size)).reshape(lines, packed))

    def with_small(value):
        return jnp.concatenate([value, small.astype(bf16)], axis=0)

    def apart(value):
        return value[:-lines], value[-lines:].astype(f32)

    kv_mine, kv_other = (
        matmul_tn(take(input_flat, at, half, 1), grad_kv).astype(bf16) for at in (c, 1 - c)
    )
    kv_other, came_small = apart(lanes.core(with_small(kv_other)))
    small = as_sent(small + came_small)
    kv_terms = [[take(part, place, depth, 0) for part in (kv_mine, kv_other)] for place in places]
    while len(kv_terms) > 1:
        count = len(kv_terms) // 2
        message = join([low_total(terms) for terms in kv_terms[count:]], 0)
        came, came_small = apart(lanes.seq(with_small(message), count.bit_length() - 1))
        small = as_sent(small + came_small)
        kv_terms = [terms + [came[p * depth : (p + 1) * depth]] for p, terms in enumerate(kv_terms[:count])]
    kv_part = low_total(kv_terms[0])
    low_small = small.astype(bf16).reshape(-1, 2 * kv_cut)
    kv_pieces = [
        jnp.concatenate(
            [
                take(part, (z + m) % n_heads, kv_cut, 1)
                for part in (kv_part[:, :kv_width], kv_part[:, kv_width:])
            ],
            axis=1,
        )
        for m in range(n_heads)
    ]
    came = lanes.direct(
        [jnp.concatenate([part, low_small], axis=0) for part in kv_pieces[1:]], True
    )
    kv_total = total_of([kv_pieces[0]] + [part[:depth] for part in came])
    sums = total_of([low_small] + [part[depth:] for part in came])
    sums = sums.reshape(-1)
    residual_grad = grad_stream + norm_back(first_back, first_normed, first_scale, first_gain)

    query_sum, output_sum = (low_total(terms) for terms in qo_scatter.terms())
    gate_grad, up_grad = (total_of(terms)[:, :units] for terms in both_scatter.terms())
    qo_parts = [
        jnp.concatenate(pair, axis=1)
        for pair in zip(split(query_sum, n_heads, 1), split(output_sum, n_heads, 1))
    ]
    qo_grad = total_of(qo_parts[:1] + lanes.direct(qo_parts[1:], True))
    query_weight_grad = qo_grad[:, :q_own]
    output_weight_grad = qo_grad[:, q_own:].T

    gain_piece = width // (lax.axis_size("dp") * n_seq * n_heads)
    gain_at = (piece * n_heads + z) * gain_piece
    attn_gain_grad = lax.dynamic_slice_in_dim(sums, gain_at, gain_piece, 0)
    ffn_gain_grad = lax.dynamic_slice_in_dim(sums, width + gain_at, gain_piece, 0)
    query_bias_grad = lax.dynamic_slice_in_dim(sums, 2 * width + z * q_own, q_own, 0)
    kv_at = 2 * width + q_all + z * kv_cut
    key_bias_grad = lax.dynamic_slice_in_dim(sums, kv_at, kv_cut, 0)
    value_bias_grad = lax.dynamic_slice_in_dim(sums, kv_at + kv_width, kv_cut, 0)

    return (
        block_out.astype(bf16),
        residual_grad.reshape(rows, own, width),
        attn_gain_grad,
        query_weight_grad,
        query_bias_grad,
        kv_total[:, :kv_cut],
        key_bias_grad,
        kv_total[:, kv_cut:],
        value_bias_grad,
        output_weight_grad,
        ffn_gain_grad,
        gate_grad,
        up_grad,
        down_grad.T,
    )


def solution(mesh):
    in_specs = (
        P("dp", ("seq", "heads"), None),
        P("dp", "seq", None),
        P("dp"),
        P(),
        P(None, "heads"),
        P("heads"),
        P(),
        P(),
        P(),
        P(),
        P("heads", None),
        P(),
        P(("dp", "seq"), "heads"),
        P(("dp", "seq"), "heads"),
        P("heads", ("dp", "seq")),
    )
    out_specs = (
        P("dp", ("seq", "heads"), None),
        P("dp", ("seq", "heads"), None),
        P(("dp", "seq", "heads")),
        P(("dp", "seq"), "heads"),
        P("heads"),
        P(("dp", "seq"), "heads"),
        P("heads"),
        P(("dp", "seq"), "heads"),
        P("heads"),
        P("heads", ("dp", "seq")),
        P(("dp", "seq", "heads")),
        P(("dp", "seq"), "heads"),
        P(("dp", "seq"), "heads"),
        P("heads", ("dp", "seq")),
    )
    return jax.shard_map(local, mesh=mesh, in_specs=in_specs, out_specs=out_specs, check_vma=False)
```
